768 devices in a mesh: face: 16 (over y, core), blk: 48 (over z, x).
Axes of the slice: x: 4, y: 8, z: 12, core: 2. Of those that a mesh axis runs over, the one named last changes fastest.
Arguments:
- isotope_ratios: float32 [3, 32, 256, 6144], P(None, None, 'face', 'blk'), may hold values from 2 to 4
- advecting_velocity: float32 [2, 32, 256, 6144], P(None, None, 'face', 'blk'), may hold values from -1 to 1
- metric_scaling: float32 [256, 6144], P('face', 'blk'), may hold values from 0.5 to 2
- thermal_state: float32 [16, 32, 55296], P('face', None, 'blk'), may hold values from 255 to 300
- outgoing_site_order: int32 [16, 55296], P('face', 'blk'), may hold values from 0 to 1151, as said below
- daytime_indicator: int32 [16, 55296], P('face', 'blk'), may hold values from 0 to 1, as said below
Outputs:
- new_tracers: float32 [3, 32, 256, 6144], P(None, None, 'face', 'blk')
- phys_tracers: float32 [16, 3, 32, 55296], P('face', None, None, 'blk')
The draws below stay inside these ranges and needn't reach their ends.
Inputs may be any that keep to these rules, and one draw needn't show every extreme that they name: `outgoing_site_order`: the 1152 entries that belong to one device are a permutation of 0 .. 1151; the device's entries k of its block name the local column it sends in position k, to blk peer k // 24. `daytime_indicator`: each device sends the same number of day columns to every peer along blk, and every physics batch (the 1152 columns one device receives) holds exactly 576 day columns.
All inputs are finite; a program needn't handle non-finite values.
Results may differ from the reference program's by a relative error of at most 0.0003.
Values sent between devices are 32-bit elements; how exact they have to be, the bound alone decides.
A program may use at most 32 MiB of HBM per device.

```python
import math
import jax
import jax.numpy as jnp
import numpy as np
from jax import lax

EX = 4
EY = 32
HEIGHT_LAYERS = 32
PARTS_ON_SQUARE = 16
PARTS_ALONG_SPAN = 48
NXN = 256
NYN = 6144
PROCESSOR_SITES = 1152
PEERCOLS = 24
SITES_PER_STRIP = 55296


def permute_columns(item_key):
    return jax.random.permutation(item_key, PROCESSOR_SITES).astype(jnp.int32)


def permute_block(item_key):
    return jax.random.permutation(item_key, PEERCOLS).astype(jnp.int32)


def column_plan(key):
    base = jax.random.fold_in(key, 7001)
    perm_keys = jax.random.split(jax.random.fold_in(base, 1), PARTS_ON_SQUARE * PARTS_ALONG_SPAN)
    send_perm = jax.vmap(permute_columns)(perm_keys).reshape(PARTS_ON_SQUARE, PARTS_ALONG_SPAN, PROCESSOR_SITES)
    half_count = jax.random.randint(jax.random.fold_in(base, 2), (PARTS_ON_SQUARE, PARTS_ALONG_SPAN // 2), 0, PEERCOLS + 1).astype(jnp.int32)
    day_count = jnp.concatenate([half_count, PEERCOLS - half_count], axis=1)
    rank_keys = jax.random.split(jax.random.fold_in(base, 3), PARTS_ON_SQUARE * PARTS_ALONG_SPAN * PARTS_ALONG_SPAN)
    ranks = jax.vmap(permute_block)(rank_keys).reshape(PARTS_ON_SQUARE, PARTS_ALONG_SPAN, PROCESSOR_SITES)
    send_day = (ranks < day_count[:, :, None]).astype(jnp.int32)
    inverse = jnp.argsort(send_perm, axis=-1).astype(jnp.int32)
    illuminated = jnp.take_along_axis(send_day, inverse, axis=-1)
    return (send_perm.reshape(PARTS_ON_SQUARE, PARTS_ALONG_SPAN * PROCESSOR_SITES), illuminated.reshape(PARTS_ON_SQUARE, PARTS_ALONG_SPAN * PROCESSOR_SITES))


def draw_outgoing_site_order(key, part):
    return column_plan(key)[0]


def draw_daytime_indicator(key, part):
    return column_plan(key)[1]


def steps_of(rng, extent, pieces, least, high):
    def one(dim, shards_of):
        steps = jax.random.uniform(jax.random.fold_in(jax.random.fold_in(rng, 6), dim), (shards_of,), jnp.float32, least / len(pieces), high / len(pieces))
        return jnp.repeat(jnp.exp(steps), extent[dim] // shards_of).reshape((-1,) + (1,) * (len(extent) - dim - 1))

    factor_of = one(*pieces[0])
    for cut in pieces[1:]:
        factor_of = factor_of * one(*cut)
    return factor_of


def setup_inputs(seed: int = 0) -> dict:
    seeds = jax.random.split(jax.random.key(seed), 7)
    return {
        "isotope_ratios": jnp.clip(2.0 + 2.0 * jax.random.uniform(seeds[0], (3, HEIGHT_LAYERS, NXN, NYN), jnp.float32) ** steps_of(seeds[0], (3, HEIGHT_LAYERS, NXN, NYN), ((2, 16), (3, 48)), -0.2, 0.2), 2.0, 4.0),
        "advecting_velocity": jnp.clip(jax.random.uniform(seeds[1], (2, HEIGHT_LAYERS, NXN, NYN), jnp.float32, -1.0, 1.0) * steps_of(seeds[1], (2, HEIGHT_LAYERS, NXN, NYN), ((2, 16), (3, 48)), -0.4, 0.0), -1.0, 1.0),
        "metric_scaling": jnp.clip(jnp.exp(math.log(2.0) - 1.3862944 * jax.random.uniform(seeds[2], (NXN, NYN), jnp.float32) ** steps_of(seeds[2], (NXN, NYN), ((0, 16), (1, 48)), -0.2, 0.2)), 0.5, 2.0),
        "thermal_state": jnp.clip(255.0 + 45.0 * jax.random.uniform(seeds[3], (PARTS_ON_SQUARE, HEIGHT_LAYERS, SITES_PER_STRIP), jnp.float32) ** steps_of(seeds[3], (PARTS_ON_SQUARE, HEIGHT_LAYERS, SITES_PER_STRIP), ((0, 16), (2, 48)), -0.2, 0.2), 255.0, 300.0),
        "outgoing_site_order": draw_outgoing_site_order(jax.random.fold_in(seeds[6], 71), 0),
        "daytime_indicator": draw_daytime_indicator(jax.random.fold_in(seeds[6], 71), 0),
    }


time_step = 0.006
absorb_coef = 0.02
heat_gain = 100.0
sat_base = 3.0
clausius = 0.07
ref_temp = 280.0

def gll_tables():
    inv_root = 1.0 / math.sqrt(5.0)
    gll_nodes = np.array([-1.0, -inv_root, inv_root, 1.0])
    legendre = (5.0 * gll_nodes ** 3 - 3.0 * gll_nodes) / 2.0
    deriv_matrix = np.zeros((4, 4))
    for row_index in range(4):
        for col_index in range(4):
            if row_index != col_index:
                deriv_matrix[row_index, col_index] = legendre[row_index] / (legendre[col_index] * (gll_nodes[row_index] - gll_nodes[col_index]))
    deriv_matrix[0, 0] = -3.0
    deriv_matrix[3, 3] = 3.0
    weights = np.array([1.0, 5.0, 5.0, 1.0]) / 6.0
    return (deriv_matrix, weights)

def derive_first(field, deriv):
    shaped = field.reshape(field.shape[0], field.shape[1] // 4, 4, field.shape[2])
    result = jnp.einsum('ij,lejy->leiy', deriv, shaped, precision=lax.Precision.HIGHEST)
    return result.reshape(field.shape)

def derive_second(field, deriv):
    shaped = field.reshape(field.shape[0], field.shape[1], field.shape[2] // 4, 4)
    result = jnp.einsum('ij,lxej->lxei', deriv, shaped, precision=lax.Precision.HIGHEST)
    return result.reshape(field.shape)

def add_partners(values, axis_dim):
    span_len = values.shape[axis_dim]
    bcast_shape = [1] * values.ndim
    bcast_shape[axis_dim] = span_len
    position = (jnp.arange(span_len) % 4).reshape(bcast_shape)
    following = jnp.roll(values, -1, axis_dim)
    before = jnp.roll(values, 1, axis_dim)
    return values + jnp.where(position == 3, following, 0.0) + jnp.where(position == 0, before, 0.0)

def radiative_warming(vapour):
    depth = jnp.cumsum(absorb_coef * vapour, axis=0)
    return heat_gain * absorb_coef * vapour * jnp.exp(-depth)

def condense(vapour, heavy, deuter, warmed_profiles):
    saturation = sat_base * jnp.exp(clausius * (warmed_profiles - ref_temp))
    remain = jnp.minimum(vapour, saturation)
    log_ratio = jnp.log(remain / vapour)
    inverse = 1.0 / warmed_profiles
    alpha_heavy = jnp.exp(1137.0 * inverse * inverse - 0.4156 * inverse - 0.0020667)
    alpha_deut = jnp.exp(24844.0 * inverse * inverse - 76.248 * inverse + 0.052612)
    return jnp.stack([remain, heavy * jnp.exp(alpha_heavy * log_ratio), deuter * jnp.exp(alpha_deut * log_ratio)])

def reference(isotope_ratios, advecting_velocity, metric_scaling, thermal_state, outgoing_site_order, daytime_indicator):
    deriv_np, weight_np = gll_tables()
    deriv = jnp.asarray(deriv_np, jnp.float32)
    size_x, size_y = metric_scaling.shape
    outer_weight = np.outer(np.tile(weight_np, size_x // 4), np.tile(weight_np, size_y // 4))
    node_mass = jnp.asarray(outer_weight, jnp.float32) * metric_scaling

    def tendency_of(tracer):
        flux_x = metric_scaling * advecting_velocity[0] * tracer
        flux_y = metric_scaling * advecting_velocity[1] * tracer
        return -(derive_first(flux_x, deriv) + derive_second(flux_y, deriv)) / metric_scaling
    tendency = lax.map(tendency_of, isotope_ratios)
    numer = add_partners(add_partners(node_mass * tendency, 2), 3)
    denom = add_partners(add_partners(node_mass, 0), 1)
    new_tracers = isotope_ratios + time_step * (numer / denom)
    shaped = new_tracers.reshape(3, HEIGHT_LAYERS, PARTS_ON_SQUARE, EX, 4, PARTS_ALONG_SPAN, EY, 4)[:, :, :, :, :3, :, :, :3]
    profile_list = shaped.transpose(0, 1, 2, 5, 3, 4, 6, 7).reshape(3, HEIGHT_LAYERS, PARTS_ON_SQUARE, PARTS_ALONG_SPAN, PROCESSOR_SITES)
    profile_warmth = thermal_state.reshape(PARTS_ON_SQUARE, HEIGHT_LAYERS, PARTS_ALONG_SPAN, PROCESSOR_SITES).transpose(1, 0, 2, 3)
    illuminated = daytime_indicator.reshape(PARTS_ON_SQUARE, PARTS_ALONG_SPAN, PROCESSOR_SITES)
    warmed_profiles = profile_warmth + jnp.where(illuminated[None] == 1, radiative_warming(profile_list[0]), 0.0)
    physics = condense(profile_list[0], profile_list[1], profile_list[2], warmed_profiles)
    send_perm = outgoing_site_order.reshape(PARTS_ON_SQUARE, PARTS_ALONG_SPAN, PROCESSOR_SITES)
    sent = jnp.take_along_axis(physics, jnp.broadcast_to(send_perm[None, None], physics.shape), axis=-1)
    sent = sent.reshape(3, HEIGHT_LAYERS, PARTS_ON_SQUARE, PARTS_ALONG_SPAN, PARTS_ALONG_SPAN, PEERCOLS).transpose(0, 1, 2, 4, 3, 5)
    sent = sent.reshape(3, HEIGHT_LAYERS, PARTS_ON_SQUARE, PARTS_ALONG_SPAN * PROCESSOR_SITES)
    return (new_tracers, sent.transpose(2, 0, 1, 3))
```

```python
import functools
import math

import jax
import jax.numpy as jnp
import numpy as np
from jax import lax
from jax.experimental import pallas as pl
from jax.experimental.pallas import tpu as pltpu
from jax.sharding import PartitionSpec as P

time_step = 0.006
absorb_coef = 0.02
heat_gain = 100.0
sat_base = 3.0
clausius = 0.07
ref_temp = 280.0

MESH = pl.DeviceIdType.MESH
F32, BF16 = jnp.float32, jnp.bfloat16
NZ, NX = 12, 4
NB = NZ * NX
ROWS, LANES, LEV = 16, 128, 32
C = 3 * LEV
CM = C + 8
SITES, PEER = 1152, 24
MSG = 18
KEEP = [ix for ix in range(ROWS) if ix % 4 != 3]


def gll_tables():
    inv_root = 1.0 / math.sqrt(5.0)
    gll_nodes = np.array([-1.0, -inv_root, inv_root, 1.0])
    legendre = (5.0 * gll_nodes**3 - 3.0 * gll_nodes) / 2.0
    deriv_matrix = np.zeros((4, 4))
    for row_index in range(4):
        for col_index in range(4):
            if row_index != col_index:
                deriv_matrix[row_index, col_index] = legendre[row_index] / (
                    legendre[col_index] * (gll_nodes[row_index] - gll_nodes[col_index])
                )
    deriv_matrix[0, 0] = -3.0
    deriv_matrix[3, 3] = 3.0
    weights = np.array([1.0, 5.0, 5.0, 1.0]) / 6.0
    return (deriv_matrix, weights)


DERIV, WEIGHT = gll_tables()


def lane_matrix():
    kron = np.kron(np.eye(LANES // 4), (-WEIGHT[:, None] * DERIV)).T
    hi = kron.astype(jnp.bfloat16).astype(np.float32)
    lo = kron.astype(np.float32) - hi
    full = np.block([[hi, lo], [hi, np.zeros_like(lo)]])
    return full.astype(jnp.bfloat16)


def expand_matrix():
    out = np.zeros((384, 512), np.float32)
    for row in range(4):
        for lane in range(LANES):
            if lane % 4 != 3:
                out[96 * row + 3 * (lane // 4) + lane % 4, 128 * row + lane] = 1.0
    return out.astype(jnp.bfloat16)


def split(x):
    hi = x.astype(BF16)
    return hi, (x - hi.astype(F32)).astype(BF16)


def mm(a, b):
    return jnp.dot(a, b, preferred_element_type=F32)


def step_kernel(
    r_hbm, v_hbm, m_hbm, t_hbm, o_hbm, d_hbm, k_hbm, e_hbm,
    nt_hbm, ph_hbm,
    r_s, v_s, m_s, t_s, o_s, d_s, k_s, e_s,
    w_s, edge_s, hx_s, he_s, nt_s, tg_s, dg_s, oh_s, xt_s, s_s, rc_s, ph_s,
    in_sem, out_sem, hsend, hrecv, ssem, rsem,
):
    f, b = lax.axis_index("face"), lax.axis_index("blk")
    nf = lax.axis_size("face")
    z, x = b // NX, b % NX
    fp, fn = (f + nf - 1) % nf, (f + 1) % nf
    bp, bn = (b + NB - 1) % NB, (b + 1) % NB

    loads = [
        pltpu.make_async_copy(src, dst, in_sem.at[i])
        for i, (src, dst) in enumerate(
            [(r_hbm, r_s), (v_hbm, v_s), (m_hbm, m_s), (k_hbm, k_s), (o_hbm, o_s), (t_hbm, t_s), (d_hbm, d_s), (e_hbm, e_s)]
        )
    ]
    for cp in loads:
        cp.start()

    barrier = pltpu.get_barrier_semaphore()
    halo = [(fp, b), (fn, b), (f, bp), (f, bn), (fp, bp), (fp, bn), (fn, bp), (fn, bn)]

    def greet(i, carry):
        pl.semaphore_signal(barrier, inc=1, device_id=(f, (b + i) % NB), device_id_type=MESH)
        return carry

    lax.fori_loop(1, NB, greet, 0)
    for peer in halo[:2] + halo[4:]:
        pl.semaphore_signal(barrier, inc=1, device_id=peer, device_id_type=MESH)

    lane = lax.broadcasted_iota(jnp.int32, (8, LANES), 1)
    wy = jnp.where((lane % 4 == 0) | (lane % 4 == 3), F32(WEIGHT[0]), F32(WEIGHT[1]))
    for cp in loads[:4]:
        cp.wait()

    for e in range(ROWS // 4):
        fx, fy = [], []
        for i in range(4):
            ix = 4 * e + i
            q = r_s[pl.ds(ix, C, stride=ROWS), :].reshape(3, LEV, LANES)
            met = m_s[ix : ix + 1, :]
            ax = v_s[pl.ds(ix, LEV, stride=ROWS), :] * met
            ay = v_s[pl.ds(LEV * ROWS + ix, LEV, stride=ROWS), :] * met
            fx.append((ax[None] * q).reshape(C, LANES))
            fy.append((ay[None] * q).reshape(C, LANES))
        hi, lo = split(jnp.concatenate(fy, axis=0))
        gy = mm(jnp.concatenate([hi, lo], axis=1), k_s[...])
        gy = gy[:, :LANES] + gy[:, LANES:]
        for i in range(4):
            gx = None
            for j in range(4):
                if DERIV[i, j] != 0.0:
                    term = F32(-WEIGHT[i] * DERIV[i, j]) * fx[j]
                    gx = term if gx is None else gx + term
            w_s[4 * e + i, :C, :] = F32(WEIGHT[i]) * gy[C * i : C * (i + 1)] + wy[:1] * gx
            w_s[4 * e + i, C:, :] = F32(WEIGHT[i]) * wy * m_s[4 * e + i : 4 * e + i + 1, :]

    for e in range(1, ROWS // 4):
        both = w_s[4 * e - 1] + w_s[4 * e]
        w_s[4 * e - 1] = both
        w_s[4 * e] = both
    edge = [jnp.zeros((8, LANES), F32) for _ in range(4)]
    for ix in range(ROWS):
        for v in range(CM // 8):
            g, rv = (v // 3, v % 3) if v < 12 else (0, 3)
            tile = w_s[ix, 8 * v : 8 * v + 8, :]
            moved = pltpu.roll(tile, (1 + 2 * ix + 32 * g) % LANES, 1)
            edge[rv] = jnp.where(lane // 2 == ix + 16 * g, moved, edge[rv])
    for rv in range(4):
        edge_s[8 * rv : 8 * rv + 8, :] = edge[rv]

    pl.semaphore_wait(barrier, NB - 1 + 6)

    def halo_copy(n):
        src = w_s.at[0] if n == 0 else w_s.at[ROWS - 1] if n == 1 else edge_s
        slot = [1, 0, 3, 2, 7, 6, 5, 4][n]
        dst = hx_s.at[slot] if n < 2 else he_s.at[slot - 2]
        return pltpu.make_async_remote_copy(
            src, dst, hsend.at[n], hrecv.at[slot], device_id=halo[n], device_id_type=MESH
        )

    def halo_wait(slot):
        dst = hx_s.at[slot] if slot < 2 else he_s.at[slot - 2]
        pltpu.make_async_remote_copy(
            dst, dst, hsend.at[slot], hrecv.at[slot], device_id=halo[slot], device_id_type=MESH
        ).wait_recv()

    for n in (7, 6, 5, 4, 1, 0, 3, 2):
        halo_copy(n).start()

    for cp in loads[4:]:
        cp.wait()
    warm = [t_s[:, 384 * k : 384 * k + 384] - F32(ref_temp) for k in range(3)]
    warm = jnp.concatenate(warm, axis=0)
    w_hi, w_lo = split(warm)
    w_lo2 = (warm - w_hi.astype(F32) - w_lo.astype(F32)).astype(BF16)
    day = [jnp.broadcast_to(d_s[:, 384 * k : 384 * k + 384].astype(F32), (16, 384)) for k in range(3)]
    day = jnp.concatenate(day, axis=0).astype(BF16)
    grid = mm(jnp.concatenate([w_hi, w_lo, w_lo2, day], axis=0), e_s[...])
    heat = grid[:C] + grid[C : 2 * C] + grid[2 * C : 3 * C] + F32(ref_temp)
    for k in range(3):
        for i in range(4):
            tg_s[4 * k + i] = heat[LEV * k : LEV * (k + 1), LANES * i : LANES * (i + 1)]
            dg_s[4 * k + i] = grid[3 * C + 16 * k : 3 * C + 16 * k + 8, LANES * i : LANES * (i + 1)]

    site = jnp.where(lane % 4 == 3, -4096, 3 * (lane // 4) + lane % 4)[:1]
    for k in range(SITES // LANES):
        want = jnp.broadcast_to(o_s[:, LANES * k : LANES * (k + 1)], (LANES, LANES)).T
        for j in range(12):
            oh_s[LANES * k : LANES * (k + 1), LANES * j : LANES * (j + 1)] = jnp.where(
                want == site + 96 * j, F32(1.0), F32(0.0)
            ).astype(BF16)

    for slot in range(8):
        halo_wait(slot)

    pos = lane % 32
    add = []
    for rv in range(4):
        rows = pl.ds(8 * rv, 8)
        prev, nxt = he_s[0, rows, :], he_s[1, rows, :]
        c = jnp.where(pos % 2 == 1, pltpu.roll(prev, 1, 1), pltpu.roll(nxt, LANES - 1, 1))
        pp, pn, np_, nn = [he_s[2 + n, rows, :] for n in range(4)]
        zero = jnp.zeros_like(c)
        c = c + jnp.where(pos == 1, pltpu.roll(pp, LANES - 29, 1), zero)
        c = c + jnp.where(pos == 0, pltpu.roll(pn, LANES - 31, 1), zero)
        c = c + jnp.where(pos == 31, pltpu.roll(np_, 31, 1), zero)
        c = c + jnp.where(pos == 30, pltpu.roll(nn, 29, 1), zero)
        add.append(c)

    def finish_row(ix):
        tiles = []
        for v in range(CM // 8):
            g, rv = (v // 3, v % 3) if v < 12 else (0, 3)
            s = w_s[ix, 8 * v : 8 * v + 8, :]
            if ix == 0:
                s = s + hx_s[0, 8 * v : 8 * v + 8, :]
            if ix == ROWS - 1:
                s = s + hx_s[1, 8 * v : 8 * v + 8, :]
            far = pltpu.roll(add[rv], (2 * LANES - (2 * ix + 1 + 32 * g)) % LANES, 1)
            other = jnp.where(
                lane % 4 == 3,
                pltpu.roll(s, LANES - 1, 1),
                jnp.where(lane % 4 == 0, pltpu.roll(s, 1, 1), F32(0.0)),
            )
            other = jnp.where((lane == 0) | (lane == LANES - 1), far, other)
            tiles.append(s + other)
        rate = F32(time_step) / tiles[12]
        q = r_s[pl.ds(ix, C, stride=ROWS), :]
        new = q + jnp.concatenate([t * rate for t in tiles[:12]], axis=0)
        nt_s[pl.ds(ix, C, stride=ROWS), :] = new
        return new

    level = lax.broadcasted_iota(jnp.int32, (LEV, LANES), 0)

    def physics(j, new):
        vapour, heavy, deuter = new[:LEV], new[LEV : 2 * LEV], new[2 * LEV :]
        depth = F32(absorb_coef) * vapour
        for shift in (1, 2, 4, 8, 16):
            depth = depth + jnp.where(level >= shift, pltpu.roll(depth, shift, 0), F32(0.0))
        heating = F32(heat_gain * absorb_coef) * vapour * jnp.exp(-depth)
        warmed = tg_s[j] + jnp.where(dg_s[j][:1] == 1.0, heating, F32(0.0))
        saturation = F32(sat_base) * jnp.exp(F32(clausius) * (warmed - F32(ref_temp)))
        remain = jnp.minimum(vapour, saturation)
        log_ratio = jnp.log(remain / vapour)
        inverse = 1.0 / warmed
        alpha_heavy = jnp.exp(F32(1137.0) * inverse * inverse - F32(0.4156) * inverse - F32(0.0020667))
        alpha_deut = jnp.exp(F32(24844.0) * inverse * inverse - F32(76.248) * inverse + F32(0.052612))
        out = [remain, heavy * jnp.exp(alpha_heavy * log_ratio), deuter * jnp.exp(alpha_deut * log_ratio)]
        out = jnp.concatenate(out + [jnp.zeros((LEV, LANES), F32)], axis=0).T
        hi, lo = split(out)
        xt_s[LANES * j : LANES * (j + 1), :LANES] = hi
        xt_s[LANES * j : LANES * (j + 1), LANES:] = lo

    for j, ix in enumerate(KEEP):
        physics(j, finish_row(ix))

    row8 = lax.broadcasted_iota(jnp.int32, (1, 8, LANES), 1)
    lane8 = lax.broadcasted_iota(jnp.int32, (1, 8, LANES), 2)
    top, late = row8 >= 2, lane8 >= C

    def send_copy(p, slot):
        return pltpu.make_async_remote_copy(
            s_s.at[p], rc_s.at[slot], ssem.at[p], rsem.at[slot], device_id=(f, p), device_id_type=MESH
        )

    def send(n, carry):
        k = 6 - n
        zs = [(z + k) % NZ, (z + NZ + 1 - k) % NZ]
        lhs = [oh_s[pl.ds(pl.multiple_of(zz * 96, 96), 96), :] for zz in zs]
        y = mm(jnp.concatenate(lhs, axis=0), xt_s[...])
        y = (y[:, :LANES] + y[:, LANES:]).reshape(8, PEER, LANES)
        v0, v1, v2 = y[:, 0:8], y[:, 8:16], y[:, 16:24]
        a0, a1, a2 = pltpu.roll(v2, 96, 2), pltpu.roll(v2, 64, 2), pltpu.roll(v2, 32, 2)
        v0 = jnp.where(late, jnp.where(top, a0, pltpu.roll(a2, 6, 1)), v0)
        v1 = jnp.where(late, jnp.where(top, a1, pltpu.roll(a2, 4, 1)), v1)
        v2 = jnp.where(late, pltpu.roll(a2, 2, 1), v2)
        for h in range(2):
            rows = pl.ds(zs[h] * NX, NX)
            s_s[rows, 0:8, :] = v0[4 * h : 4 * h + 4]
            s_s[rows, 8:16, :] = v1[4 * h : 4 * h + 4]
            s_s[rows, 16:18, :] = v2[4 * h : 4 * h + 4, 0:2]
        for h in range(2):
            for xx in range(NX):
                p = zs[h] * NX + (x + xx) % NX

                @pl.when(p != b)
                def _():
                    send_copy(p, b).start()

        return carry

    lax.fori_loop(0, NZ // 2, send, 0)
    rc_s[b] = s_s[b]

    for ix in range(3, ROWS, 4):
        finish_row(ix)
    out_nt = pltpu.make_async_copy(nt_s, nt_hbm, out_sem.at[0])
    out_nt.start()
    for n in range(8):
        halo_copy(n).wait_send()

    outs = []
    for g in range(3):
        def arrive(i, carry):
            p = 16 * g + i

            @pl.when(p != b)
            def _():
                send_copy(p, p).wait_recv()

            return carry

        lax.fori_loop(0, 16, arrive, 0)
        grp = pl.ds(16 * g, 16)
        v0, v1 = rc_s[grp, 0:8, :], rc_s[grp, 8:16, :]
        v2 = jnp.concatenate([rc_s[grp, 16:18, :], jnp.zeros((16, 6, LANES), F32)], axis=1)
        a2 = jnp.where(
            row8 < 4, pltpu.roll(v0, 2, 1), jnp.where(row8 < 6, pltpu.roll(v1, 4, 1), pltpu.roll(v2, 6, 1))
        )
        tail = jnp.where(
            lane8 < 32, pltpu.roll(v0, 32, 2), jnp.where(lane8 < 64, pltpu.roll(v1, 64, 2), pltpu.roll(a2, 96, 2))
        )
        v2 = jnp.where(top, tail, v2)
        cols = jnp.concatenate([v0, v1, v2], axis=1).reshape(16 * PEER, LANES)
        ph_s[:, 384 * g : 384 * (g + 1)] = cols.T[:C]
        outs.append(
            pltpu.make_async_copy(
                ph_s.at[:, pl.ds(384 * g, 384)], ph_hbm.at[:, pl.ds(384 * g, 384)], out_sem.at[1 + g]
            )
        )
        outs[-1].start()

    def drain(i, carry):
        @pl.when(i != b)
        def _():
            send_copy(i, b).wait_send()

        return carry

    lax.fori_loop(0, NB, drain, 0)
    for cp in [out_nt] + outs:
        cp.wait()


def on_device(isotope_ratios, advecting_velocity, metric_scaling, thermal_state, outgoing_site_order, daytime_indicator):
    hbm = pl.BlockSpec(memory_space=pltpu.HBM)
    vm = lambda *shape, dtype=F32: pltpu.VMEM(shape, dtype)
    new_tracers, physics = pl.pallas_call(
        step_kernel,
        out_shape=(
            jax.ShapeDtypeStruct((C * ROWS, LANES), F32),
            jax.ShapeDtypeStruct((C, SITES), F32),
        ),
        in_specs=[hbm] * 8,
        out_specs=(hbm, hbm),
        scratch_shapes=[
            vm(C * ROWS, LANES), vm(2 * LEV * ROWS, LANES), vm(ROWS, LANES), vm(LEV, SITES),
            vm(1, SITES, dtype=jnp.int32), vm(1, SITES, dtype=jnp.int32),
            vm(2 * LANES, 2 * LANES, dtype=BF16), vm(384, 512, dtype=BF16),
            vm(ROWS, CM, LANES), vm(LEV, LANES), vm(2, CM, LANES), vm(6, LEV, LANES),
            vm(C * ROWS, LANES), vm(12, LEV, LANES), vm(12, 8, LANES),
            vm(SITES, 12 * LANES, dtype=BF16), vm(12 * LANES, 2 * LANES, dtype=BF16),
            vm(NB, MSG, LANES), vm(NB, MSG, LANES), vm(C, SITES),
            pltpu.SemaphoreType.DMA((8,)), pltpu.SemaphoreType.DMA((4,)),
            pltpu.SemaphoreType.DMA((8,)), pltpu.SemaphoreType.DMA((8,)),
            pltpu.SemaphoreType.DMA((NB,)), pltpu.SemaphoreType.DMA((NB,)),
        ],
        compiler_params=pltpu.CompilerParams(
            collective_id=0, has_side_effects=True, vmem_limit_bytes=48 * 1024 * 1024
        ),
        name="transport_condense",
    )(
        isotope_ratios.reshape(C * ROWS, LANES),
        advecting_velocity.reshape(2 * LEV * ROWS, LANES),
        metric_scaling,
        thermal_state[0],
        outgoing_site_order,
        daytime_indicator,
        jnp.asarray(lane_matrix()),
        jnp.asarray(expand_matrix()),
    )
    return (new_tracers.reshape(3, LEV, ROWS, LANES), physics.reshape(1, 3, LEV, SITES))


def solution(mesh):
    placed = (
        P(None, None, "face", "blk"),
        P(None, None, "face", "blk"),
        P("face", "blk"),
        P("face", None, "blk"),
        P("face", "blk"),
        P("face", "blk"),
    )
    return jax.shard_map(
        on_device,
        mesh=mesh,
        in_specs=placed,
        out_specs=(P(None, None, "face", "blk"), P("face", None, None, "blk")),
        check_vma=False,
    )
```

```python
import functools
import math

import jax
import jax.numpy as jnp
import numpy as np
from jax import lax
from jax.experimental import pallas as pl
from jax.experimental.pallas import tpu as pltpu
from jax.sharding import PartitionSpec as P

time_step = 0.006
absorb_coef = 0.02
heat_gain = 100.0
sat_base = 3.0
clausius = 0.07
ref_temp = 280.0

MESH = pl.DeviceIdType.MESH
F32, BF16 = jnp.float32, jnp.bfloat16
NZ, NX = 12, 4
NB = NZ * NX
ROWS, LANES, LEV = 16, 128, 32
C = 3 * LEV
CM = C + 8
SITES, PEER = 1152, 24
MSG = 18
GRANT = 67043328
KEEP = [ix for ix in range(ROWS) if ix % 4 != 3]


def gll_tables():
    inv_root = 1.0 / math.sqrt(5.0)
    gll_nodes = np.array([-1.0, -inv_root, inv_root, 1.0])
    legendre = (5.0 * gll_nodes**3 - 3.0 * gll_nodes) / 2.0
    deriv_matrix = np.zeros((4, 4))
    for row_index in range(4):
        for col_index in range(4):
            if row_index != col_index:
                deriv_matrix[row_index, col_index] = legendre[row_index] / (
                    legendre[col_index] * (gll_nodes[row_index] - gll_nodes[col_index])
                )
    deriv_matrix[0, 0] = -3.0
    deriv_matrix[3, 3] = 3.0
    weights = np.array([1.0, 5.0, 5.0, 1.0]) / 6.0
    return (deriv_matrix, weights)


DERIV, WEIGHT = gll_tables()


def lane_matrix():
    kron = np.kron(np.eye(LANES // 4), (-WEIGHT[:, None] * DERIV)).T
    hi = kron.astype(jnp.bfloat16).astype(np.float32)
    lo = kron.astype(np.float32) - hi
    full = np.block([[hi, lo], [hi, np.zeros_like(lo)]])
    return full.astype(jnp.bfloat16)


def expand_matrix():
    out = np.zeros((384, 512), np.float32)
    for row in range(4):
        for lane in range(LANES):
            if lane % 4 != 3:
                out[96 * row + 3 * (lane // 4) + lane % 4, 128 * row + lane] = 1.0
    return out.astype(jnp.bfloat16)


def split(x):
    hi = x.astype(BF16)
    return hi, (x - hi.astype(F32)).astype(BF16)


def mm(a, b):
    return jnp.dot(a, b, preferred_element_type=F32)


def step_kernel(
    r_hbm, v_hbm, m_hbm, t_hbm, o_hbm, d_hbm, k_hbm, e_hbm,
    nt_s, rc_s,
    r_s, v_s, m_s, t_s, o_s, d_s, k_s, e_s,
    w_s, edge_s, hx_s, he_s, tg_s, dg_s, oh_s, xt_s, s_s,
    in_sem, hsend, hrecv, ssem, rsem, round_sem,
):
    f, b = lax.axis_index("face"), lax.axis_index("blk")
    nf = lax.axis_size("face")
    z, x = b // NX, b % NX
    fp, fn = (f + nf - 1) % nf, (f + 1) % nf
    bp, bn = (b + NB - 1) % NB, (b + 1) % NB

    loads = [
        pltpu.make_async_copy(src, dst, in_sem.at[i])
        for i, (src, dst) in enumerate(
            [(r_hbm, r_s), (v_hbm, v_s), (m_hbm, m_s), (k_hbm, k_s), (o_hbm, o_s), (t_hbm, t_s), (d_hbm, d_s), (e_hbm, e_s)]
        )
    ]
    for cp in loads:
        cp.start()

    halo = [(fp, b), (fn, b), (f, bp), (f, bn), (fp, bp), (fp, bn), (fn, bp), (fn, bn)]
    row_mates = [(f, z * NX + (x + d) % NX) for d in range(1, NX)]
    column_mates = [(f, (z + d) % NZ * NX + x) for d in (1, NZ - 1, 2, NZ - 2, 3, NZ - 3)]

    def greet(sem, peers):
        for peer in peers:
            pl.semaphore_signal(sem, inc=1, device_id=peer, device_id_type=MESH)

    barrier = pltpu.get_barrier_semaphore()
    near = column_mates[::-1] + halo + row_mates
    greet(barrier, near)

    lane = lax.broadcasted_iota(jnp.int32, (8, LANES), 1)
    wy = jnp.where((lane % 4 == 0) | (lane % 4 == 3), F32(WEIGHT[0]), F32(WEIGHT[1]))
    for cp in loads[:4]:
        cp.wait()

    for e in range(ROWS // 4):
        fx, fy = [], []
        for i in range(4):
            ix = 4 * e + i
            q = r_s[pl.ds(ix, C, stride=ROWS), :].reshape(3, LEV, LANES)
            met = m_s[ix : ix + 1, :]
            ax = v_s[pl.ds(ix, LEV, stride=ROWS), :] * met
            ay = v_s[pl.ds(LEV * ROWS + ix, LEV, stride=ROWS), :] * met
            fx.append((ax[None] * q).reshape(C, LANES))
            fy.append((ay[None] * q).reshape(C, LANES))
        hi, lo = split(jnp.concatenate(fy, axis=0))
        gy = mm(jnp.concatenate([hi, lo], axis=1), k_s[...])
        gy = gy[:, :LANES] + gy[:, LANES:]
        for i in range(4):
            gx = None
            for j in range(4):
                if DERIV[i, j] != 0.0:
                    term = F32(-WEIGHT[i] * DERIV[i, j]) * fx[j]
                    gx = term if gx is None else gx + term
            w_s[4 * e + i, :C, :] = F32(WEIGHT[i]) * gy[C * i : C * (i + 1)] + wy[:1] * gx
            w_s[4 * e + i, C:, :] = F32(WEIGHT[i]) * wy * m_s[4 * e + i : 4 * e + i + 1, :]

    for e in range(1, ROWS // 4):
        both = w_s[4 * e - 1] + w_s[4 * e]
        w_s[4 * e - 1] = both
        w_s[4 * e] = both
    edge = [jnp.zeros((8, LANES), F32) for _ in range(4)]
    for ix in range(ROWS):
        for v in range(CM // 8):
            g, rv = (v // 3, v % 3) if v < 12 else (0, 3)
            tile = w_s[ix, 8 * v : 8 * v + 8, :]
            moved = pltpu.roll(tile, (1 + 2 * ix + 32 * g) % LANES, 1)
            edge[rv] = jnp.where(lane // 2 == ix + 16 * g, moved, edge[rv])
    for rv in range(4):
        edge_s[8 * rv : 8 * rv + 8, :] = edge[rv]

    pl.semaphore_wait(barrier, len(near))
    greet(round_sem.at[0], column_mates[::-1] + row_mates)

    def halo_copy(n):
        src = w_s.at[0] if n == 0 else w_s.at[ROWS - 1] if n == 1 else edge_s
        slot = [1, 0, 3, 2, 7, 6, 5, 4][n]
        dst = hx_s.at[slot] if n < 2 else he_s.at[slot - 2]
        return pltpu.make_async_remote_copy(
            src, dst, hsend.at[n], hrecv.at[slot], device_id=halo[n], device_id_type=MESH
        )

    def halo_wait(slot):
        dst = hx_s.at[slot] if slot < 2 else he_s.at[slot - 2]
        pltpu.make_async_remote_copy(
            dst, dst, hsend.at[slot], hrecv.at[slot], device_id=halo[slot], device_id_type=MESH
        ).wait_recv()

    for n in (7, 6, 5, 4, 1, 0, 3, 2):
        halo_copy(n).start()

    for cp in loads[4:]:
        cp.wait()
    warm = [t_s[:, 384 * k : 384 * k + 384] - F32(ref_temp) for k in range(3)]
    warm = jnp.concatenate(warm, axis=0)
    w_hi, w_lo = split(warm)
    w_lo2 = (warm - w_hi.astype(F32) - w_lo.astype(F32)).astype(BF16)
    day = [jnp.broadcast_to(d_s[:, 384 * k : 384 * k + 384].astype(F32), (16, 384)) for k in range(3)]
    day = jnp.concatenate(day, axis=0).astype(BF16)
    grid = mm(jnp.concatenate([w_hi, w_lo, w_lo2, day], axis=0), e_s[...])
    heat = grid[:C] + grid[C : 2 * C] + grid[2 * C : 3 * C] + F32(ref_temp)
    for k in range(3):
        for i in range(4):
            tg_s[4 * k + i] = heat[LEV * k : LEV * (k + 1), LANES * i : LANES * (i + 1)]
            dg_s[4 * k + i] = grid[3 * C + 16 * k : 3 * C + 16 * k + 8, LANES * i : LANES * (i + 1)]

    site = jnp.where(lane % 4 == 3, -4096, 3 * (lane // 4) + lane % 4)[:1]
    for k in range(SITES // LANES):
        want = jnp.broadcast_to(o_s[:, LANES * k : LANES * (k + 1)], (LANES, LANES)).T
        for j in range(12):
            oh_s[LANES * k : LANES * (k + 1), LANES * j : LANES * (j + 1)] = jnp.where(
                want == site + 96 * j, F32(1.0), F32(0.0)
            ).astype(BF16)

    pl.semaphore_wait(round_sem.at[0], len(column_mates) + len(row_mates))
    greet(round_sem.at[1], row_mates)
    for slot in range(8):
        halo_wait(slot)

    pos = lane % 32
    add = []
    for rv in range(4):
        rows = pl.ds(8 * rv, 8)
        prev, nxt = he_s[0, rows, :], he_s[1, rows, :]
        c = jnp.where(pos % 2 == 1, pltpu.roll(prev, 1, 1), pltpu.roll(nxt, LANES - 1, 1))
        pp, pn, np_, nn = [he_s[2 + n, rows, :] for n in range(4)]
        zero = jnp.zeros_like(c)
        c = c + jnp.where(pos == 1, pltpu.roll(pp, LANES - 29, 1), zero)
        c = c + jnp.where(pos == 0, pltpu.roll(pn, LANES - 31, 1), zero)
        c = c + jnp.where(pos == 31, pltpu.roll(np_, 31, 1), zero)
        c = c + jnp.where(pos == 30, pltpu.roll(nn, 29, 1), zero)
        add.append(c)

    def finish_row(ix):
        tiles = []
        for v in range(CM // 8):
            g, rv = (v // 3, v % 3) if v < 12 else (0, 3)
            s = w_s[ix, 8 * v : 8 * v + 8, :]
            if ix == 0:
                s = s + hx_s[0, 8 * v : 8 * v + 8, :]
            if ix == ROWS - 1:
                s = s + hx_s[1, 8 * v : 8 * v + 8, :]
            far = pltpu.roll(add[rv], (2 * LANES - (2 * ix + 1 + 32 * g)) % LANES, 1)
            other = jnp.where(
                lane % 4 == 3,
                pltpu.roll(s, LANES - 1, 1),
                jnp.where(lane % 4 == 0, pltpu.roll(s, 1, 1), F32(0.0)),
            )
            other = jnp.where((lane == 0) | (lane == LANES - 1), far, other)
            tiles.append(s + other)
        rate = F32(time_step) / tiles[12]
        q = r_s[pl.ds(ix, C, stride=ROWS), :]
        new = q + jnp.concatenate([t * rate for t in tiles[:12]], axis=0)
        nt_s[pl.ds(ix, C, stride=ROWS), :] = new
        return new

    level = lax.broadcasted_iota(jnp.int32, (LEV, LANES), 0)

    def physics(j, new):
        vapour, heavy, deuter = new[:LEV], new[LEV : 2 * LEV], new[2 * LEV :]
        depth = F32(absorb_coef) * vapour
        for shift in (1, 2, 4, 8, 16):
            depth = depth + jnp.where(level >= shift, pltpu.roll(depth, shift, 0), F32(0.0))
        heating = F32(heat_gain * absorb_coef) * vapour * jnp.exp(-depth)
        warmed = tg_s[j] + jnp.where(dg_s[j][:1] == 1.0, heating, F32(0.0))
        saturation = F32(sat_base) * jnp.exp(F32(clausius) * (warmed - F32(ref_temp)))
        remain = jnp.minimum(vapour, saturation)
        log_ratio = jnp.log(remain / vapour)
        inverse = 1.0 / warmed
        alpha_heavy = jnp.exp(F32(1137.0) * inverse * inverse - F32(0.4156) * inverse - F32(0.0020667))
        alpha_deut = jnp.exp(F32(24844.0) * inverse * inverse - F32(76.248) * inverse + F32(0.052612))
        out = [remain, heavy * jnp.exp(alpha_heavy * log_ratio), deuter * jnp.exp(alpha_deut * log_ratio)]
        out = jnp.concatenate(out + [jnp.zeros((LEV, LANES), F32)], axis=0).T
        hi, lo = split(out)
        xt_s[LANES * j : LANES * (j + 1), :LANES] = hi
        xt_s[LANES * j : LANES * (j + 1), LANES:] = lo

    for j, ix in enumerate(KEEP):
        physics(j, finish_row(ix))

    row8 = lax.broadcasted_iota(jnp.int32, (1, 8, LANES), 1)
    lane8 = lax.broadcasted_iota(jnp.int32, (1, 8, LANES), 2)
    top, late = row8 >= 2, lane8 >= C

    def send_copy(p, slot):
        return pltpu.make_async_remote_copy(
            s_s.at[p], rc_s.at[slot], ssem.at[p], rsem.at[slot], device_id=(f, p), device_id_type=MESH
        )

    def send(n, carry):
        k = 6 - n
        zs = [(z + k) % NZ, (z + NZ + 1 - k) % NZ]
        lhs = [oh_s[pl.ds(pl.multiple_of(zz * 96, 96), 96), :] for zz in zs]
        y = mm(jnp.concatenate(lhs, axis=0), xt_s[...])
        y = (y[:, :LANES] + y[:, LANES:]).reshape(8, PEER, LANES)
        v0, v1, v2 = y[:, 0:8], y[:, 8:16], y[:, 16:24]
        a0, a1, a2 = pltpu.roll(v2, 96, 2), pltpu.roll(v2, 64, 2), pltpu.roll(v2, 32, 2)
        v0 = jnp.where(late, jnp.where(top, a0, pltpu.roll(a2, 6, 1)), v0)
        v1 = jnp.where(late, jnp.where(top, a1, pltpu.roll(a2, 4, 1)), v1)
        v2 = jnp.where(late, pltpu.roll(a2, 2, 1), v2)
        for h in range(2):
            rows = pl.ds(zs[h] * NX, NX)
            s_s[rows, 0:8, :] = v0[4 * h : 4 * h + 4]
            s_s[rows, 8:16, :] = v1[4 * h : 4 * h + 4]
            s_s[rows, 16:18, :] = v2[4 * h : 4 * h + 4, 0:2]
        for h in range(2):
            for xx in range(NX):
                p = zs[h] * NX + (x + xx) % NX

                @pl.when(p != b)
                def _():
                    send_copy(p, b).start()

        return carry

    pl.semaphore_wait(round_sem.at[1], len(row_mates))
    lax.fori_loop(0, NZ // 2, send, 0)
    rc_s[b] = s_s[b]

    for ix in range(3, ROWS, 4):
        finish_row(ix)
    for n in range(8):
        halo_copy(n).wait_send()

    def arrive(i, carry):
        @pl.when(i != b)
        def _():
            send_copy(i, b).wait_send()
            send_copy(i, i).wait_recv()

        return carry

    lax.fori_loop(0, NB, arrive, 0)


def write_kernel(nt_s, rc_s, nt_hbm, ph_hbm, ph_s, sem):
    out_nt = pltpu.make_async_copy(nt_s, nt_hbm, sem.at[0])
    out_nt.start()
    row8 = lax.broadcasted_iota(jnp.int32, (1, 8, LANES), 1)
    lane8 = lax.broadcasted_iota(jnp.int32, (1, 8, LANES), 2)
    outs = []
    for g in range(3):
        grp = pl.ds(16 * g, 16)
        v0, v1 = rc_s[grp, 0:8, :], rc_s[grp, 8:16, :]
        v2 = jnp.concatenate([rc_s[grp, 16:18, :], jnp.zeros((16, 6, LANES), F32)], axis=1)
        a2 = jnp.where(
            row8 < 4, pltpu.roll(v0, 2, 1), jnp.where(row8 < 6, pltpu.roll(v1, 4, 1), pltpu.roll(v2, 6, 1))
        )
        tail = jnp.where(
            lane8 < 32, pltpu.roll(v0, 32, 2), jnp.where(lane8 < 64, pltpu.roll(v1, 64, 2), pltpu.roll(a2, 96, 2))
        )
        v2 = jnp.where(row8 >= 2, tail, v2)
        cols = jnp.concatenate([v0, v1, v2], axis=1).reshape(16 * PEER, LANES)
        part = pl.ds(384 * g, 384)
        ph_s[:, part] = cols.T[:C]
        outs.append(pltpu.make_async_copy(ph_s.at[:, part], ph_hbm.at[:, part], sem.at[1 + g]))
        outs[-1].start()
    for cp in [out_nt] + outs:
        cp.wait()


def on_device(isotope_ratios, advecting_velocity, metric_scaling, thermal_state, outgoing_site_order, daytime_indicator):
    hbm = pl.BlockSpec(memory_space=pltpu.HBM)
    vm = lambda *shape, dtype=F32: pltpu.VMEM(shape, dtype)
    moved = (vm(C * ROWS, LANES), vm(NB, MSG, LANES))
    new_tracers, arrived = pl.pallas_call(
        step_kernel,
        out_shape=moved,
        in_specs=[hbm] * 8,
        out_specs=(pl.BlockSpec(memory_space=pltpu.VMEM),) * 2,
        scratch_shapes=[
            vm(C * ROWS, LANES), vm(2 * LEV * ROWS, LANES), vm(ROWS, LANES), vm(LEV, SITES),
            vm(1, SITES, dtype=jnp.int32), vm(1, SITES, dtype=jnp.int32),
            vm(2 * LANES, 2 * LANES, dtype=BF16), vm(384, 512, dtype=BF16),
            vm(ROWS, CM, LANES), vm(LEV, LANES), vm(2, CM, LANES), vm(6, LEV, LANES),
            vm(12, LEV, LANES), vm(12, 8, LANES),
            vm(SITES, 12 * LANES, dtype=BF16), vm(12 * LANES, 2 * LANES, dtype=BF16),
            vm(NB, MSG, LANES),
            pltpu.SemaphoreType.DMA((8,)),
            pltpu.SemaphoreType.DMA((8,)), pltpu.SemaphoreType.DMA((8,)),
            pltpu.SemaphoreType.DMA((NB,)), pltpu.SemaphoreType.DMA((NB,)),
            pltpu.SemaphoreType.REGULAR((2,)),
        ],
        compiler_params=pltpu.CompilerParams(
            collective_id=0, has_side_effects=True, vmem_limit_bytes=GRANT - 1536 * 1024
        ),
        name="transport_condense",
    )(
        isotope_ratios.reshape(C * ROWS, LANES),
        advecting_velocity.reshape(2 * LEV * ROWS, LANES),
        metric_scaling,
        thermal_state[0],
        outgoing_site_order,
        daytime_indicator,
        jnp.asarray(lane_matrix()),
        jnp.asarray(expand_matrix()),
    )
    new_tracers, physics = pl.pallas_call(
        write_kernel,
        out_shape=(
            jax.ShapeDtypeStruct((C * ROWS, LANES), F32),
            jax.ShapeDtypeStruct((C, SITES), F32),
        ),
        in_specs=(pl.BlockSpec(memory_space=pltpu.VMEM),) * 2,
        out_specs=(hbm, hbm),
        scratch_shapes=[vm(C, SITES), pltpu.SemaphoreType.DMA((4,))],
        compiler_params=pltpu.CompilerParams(vmem_limit_bytes=8 * 1024 * 1024),
        name="write_results",
    )(new_tracers, arrived)
    return (new_tracers.reshape(3, LEV, ROWS, LANES), physics.reshape(1, 3, LEV, SITES))


def solution(mesh):
    placed = (
        P(None, None, "face", "blk"),
        P(None, None, "face", "blk"),
        P("face", "blk"),
        P("face", None, "blk"),
        P("face", "blk"),
        P("face", "blk"),
    )
    return jax.shard_map(
        on_device,
        mesh=mesh,
        in_specs=placed,
        out_specs=(P(None, None, "face", "blk"), P("face", None, None, "blk")),
        check_vma=False,
    )
```

```python
import functools
import math

import jax
import jax.numpy as jnp
import numpy as np
from jax import lax
from jax.experimental import pallas as pl
from jax.experimental.pallas import tpu as pltpu
from jax.sharding import PartitionSpec as P

time_step = 0.006
absorb_coef = 0.02
heat_gain = 100.0
sat_base = 3.0
clausius = 0.07
ref_temp = 280.0

MESH = pl.DeviceIdType.MESH
F32, BF16 = jnp.float32, jnp.bfloat16
NZ, NX = 12, 4
NB = NZ * NX
ROWS, LANES, LEV = 16, 128, 32
C = 3 * LEV
CM = C + 8
SITES, PEER = 1152, 24
MSG = 18
GRANT = 67043328
KEEP = [ix for ix in range(ROWS) if ix % 4 != 3]


def gll_tables():
    inv_root = 1.0 / math.sqrt(5.0)
    gll_nodes = np.array([-1.0, -inv_root, inv_root, 1.0])
    legendre = (5.0 * gll_nodes**3 - 3.0 * gll_nodes) / 2.0
    deriv_matrix = np.zeros((4, 4))
    for row_index in range(4):
        for col_index in range(4):
            if row_index != col_index:
                deriv_matrix[row_index, col_index] = legendre[row_index] / (
                    legendre[col_index] * (gll_nodes[row_index] - gll_nodes[col_index])
                )
    deriv_matrix[0, 0] = -3.0
    deriv_matrix[3, 3] = 3.0
    weights = np.array([1.0, 5.0, 5.0, 1.0]) / 6.0
    return (deriv_matrix, weights)


DERIV, WEIGHT = gll_tables()


def lane_matrix():
    kron = np.kron(np.eye(LANES // 4), (-WEIGHT[:, None] * DERIV)).T
    hi = kron.astype(jnp.bfloat16).astype(np.float32)
    lo = kron.astype(np.float32) - hi
    full = np.block([[hi, lo], [hi, np.zeros_like(lo)]])
    return full.astype(jnp.bfloat16)


def expand_matrix():
    out = np.zeros((384, 512), np.float32)
    for row in range(4):
        for lane in range(LANES):
            if lane % 4 != 3:
                out[96 * row + 3 * (lane // 4) + lane % 4, 128 * row + lane] = 1.0
    return out.astype(jnp.bfloat16)


def split(x):
    hi = x.astype(BF16)
    return hi, (x - hi.astype(F32)).astype(BF16)


def mm(a, b):
    return jnp.dot(a, b, preferred_element_type=F32)


def step_kernel(
    r_hbm, v_hbm, m_hbm, t_hbm, o_hbm, d_hbm, k_hbm, e_hbm,
    nt_s, rc_s,
    r_s, v_s, m_s, t_s, o_s, d_s, k_s, e_s,
    w_s, edge_s, hx_s, he_s, tg_s, dg_s, oh_s, xt_s, s_s,
    in_sem, hsend, hrecv, ssem, rsem, round_sem,
):
    f, b = lax.axis_index("face"), lax.axis_index("blk")
    nf = lax.axis_size("face")
    z, x = b // NX, b % NX
    fp, fn = (f + nf - 1) % nf, (f + 1) % nf
    bp, bn = (b + NB - 1) % NB, (b + 1) % NB

    loads = [
        pltpu.make_async_copy(src, dst, in_sem.at[i])
        for i, (src, dst) in enumerate(
            [(r_hbm, r_s), (v_hbm, v_s), (m_hbm, m_s), (k_hbm, k_s), (o_hbm, o_s), (t_hbm, t_s), (d_hbm, d_s), (e_hbm, e_s)]
        )
    ]
    for cp in loads:
        cp.start()

    halo = [(fp, b), (fn, b), (f, bp), (f, bn), (fp, bp), (fp, bn), (fn, bp), (fn, bn)]
    row_mates = [(f, z * NX + (x + d) % NX) for d in range(1, NX)]
    column_mates = [(f, (z + d) % NZ * NX + x) for d in (1, NZ - 1, 2, NZ - 2, 3, NZ - 3)]

    def greet(sem, peers):
        for peer in peers:
            pl.semaphore_signal(sem, inc=1, device_id=peer, device_id_type=MESH)

    barrier = pltpu.get_barrier_semaphore()
    near = column_mates[::-1] + halo + row_mates
    greet(barrier, near)

    lane = lax.broadcasted_iota(jnp.int32, (8, LANES), 1)
    wy = jnp.where((lane % 4 == 0) | (lane % 4 == 3), F32(WEIGHT[0]), F32(WEIGHT[1]))
    for cp in loads[:4]:
        cp.wait()

    for e in range(ROWS // 4):
        fx, fy = [], []
        for i in range(4):
            ix = 4 * e + i
            q = r_s[pl.ds(ix, C, stride=ROWS), :].reshape(3, LEV, LANES)
            met = m_s[ix : ix + 1, :]
            ax = v_s[pl.ds(ix, LEV, stride=ROWS), :] * met
            ay = v_s[pl.ds(LEV * ROWS + ix, LEV, stride=ROWS), :] * met
            fx.append((ax[None] * q).reshape(C, LANES))
            fy.append((ay[None] * q).reshape(C, LANES))
        hi, lo = split(jnp.concatenate(fy, axis=0))
        gy = mm(jnp.concatenate([hi, lo], axis=1), k_s[...])
        gy = gy[:, :LANES] + gy[:, LANES:]
        for i in range(4):
            gx = None
            for j in range(4):
                if DERIV[i, j] != 0.0:
                    term = F32(-WEIGHT[i] * DERIV[i, j]) * fx[j]
                    gx = term if gx is None else gx + term
            w_s[4 * e + i, :C, :] = F32(WEIGHT[i]) * gy[C * i : C * (i + 1)] + wy[:1] * gx
            w_s[4 * e + i, C:, :] = F32(WEIGHT[i]) * wy * m_s[4 * e + i : 4 * e + i + 1, :]

    for e in range(1, ROWS // 4):
        both = w_s[4 * e - 1] + w_s[4 * e]
        w_s[4 * e - 1] = both
        w_s[4 * e] = both
    edge = [jnp.zeros((8, LANES), F32) for _ in range(4)]
    for ix in range(ROWS):
        for v in range(CM // 8):
            g, rv = (v // 3, v % 3) if v < 12 else (0, 3)
            tile = w_s[ix, 8 * v : 8 * v + 8, :]
            moved = pltpu.roll(tile, (1 + 2 * ix + 32 * g) % LANES, 1)
            edge[rv] = jnp.where(lane // 2 == ix + 16 * g, moved, edge[rv])
    for rv in range(4):
        edge_s[8 * rv : 8 * rv + 8, :] = edge[rv]

    pl.semaphore_wait(barrier, len(near))
    greet(round_sem.at[1], column_mates[4:])
    greet(round_sem.at[0], row_mates)

    def halo_copy(n):
        src = w_s.at[0] if n == 0 else w_s.at[ROWS - 1] if n == 1 else edge_s
        slot = [1, 0, 3, 2, 7, 6, 5, 4][n]
        dst = hx_s.at[slot] if n < 2 else he_s.at[slot - 2]
        return pltpu.make_async_remote_copy(
            src, dst, hsend.at[n], hrecv.at[slot], device_id=halo[n], device_id_type=MESH
        )

    def halo_wait(slot):
        dst = hx_s.at[slot] if slot < 2 else he_s.at[slot - 2]
        pltpu.make_async_remote_copy(
            dst, dst, hsend.at[slot], hrecv.at[slot], device_id=halo[slot], device_id_type=MESH
        ).wait_recv()

    for n in (7, 1, 3, 6, 5, 4, 0, 2):
        halo_copy(n).start()

    for cp in loads[4:]:
        cp.wait()
    warm = [t_s[:, 384 * k : 384 * k + 384] - F32(ref_temp) for k in range(3)]
    warm = jnp.concatenate(warm, axis=0)
    w_hi, w_lo = split(warm)
    w_lo2 = (warm - w_hi.astype(F32) - w_lo.astype(F32)).astype(BF16)
    day = [jnp.broadcast_to(d_s[:, 384 * k : 384 * k + 384].astype(F32), (16, 384)) for k in range(3)]
    day = jnp.concatenate(day, axis=0).astype(BF16)
    grid = mm(jnp.concatenate([w_hi, w_lo, w_lo2, day], axis=0), e_s[...])
    heat = grid[:C] + grid[C : 2 * C] + grid[2 * C : 3 * C] + F32(ref_temp)
    for k in range(3):
        for i in range(4):
            tg_s[4 * k + i] = heat[LEV * k : LEV * (k + 1), LANES * i : LANES * (i + 1)]
            dg_s[4 * k + i] = grid[3 * C + 16 * k : 3 * C + 16 * k + 8, LANES * i : LANES * (i + 1)]

    site = jnp.where(lane % 4 == 3, -4096, 3 * (lane // 4) + lane % 4)[:1]
    for k in range(SITES // LANES):
        want = jnp.broadcast_to(o_s[:, LANES * k : LANES * (k + 1)], (LANES, LANES)).T
        for j in range(12):
            oh_s[LANES * k : LANES * (k + 1), LANES * j : LANES * (j + 1)] = jnp.where(
                want == site + 96 * j, F32(1.0), F32(0.0)
            ).astype(BF16)

    pl.semaphore_wait(round_sem.at[1], 2)
    greet(round_sem.at[2], row_mates)
    for slot in (0, 2, 4):
        halo_wait(slot)

    pos = lane % 32

    def edge_lanes(whole):
        add = []
        for rv in range(4):
            rows = pl.ds(8 * rv, 8)
            before = pltpu.roll(he_s[0, rows, :], 1, 1)
            before = before + jnp.where(pos == 1, pltpu.roll(he_s[2, rows, :], LANES - 29, 1), F32(0.0))
            after = jnp.zeros_like(before)
            if whole:
                after = pltpu.roll(he_s[1, rows, :], LANES - 1, 1)
                before = before + jnp.where(pos == 31, pltpu.roll(he_s[4, rows, :], 31, 1), F32(0.0))
                after = after + jnp.where(pos == 0, pltpu.roll(he_s[3, rows, :], LANES - 31, 1), F32(0.0))
                after = after + jnp.where(pos == 30, pltpu.roll(he_s[5, rows, :], 29, 1), F32(0.0))
            add.append(jnp.where(pos % 2 == 1, before, after))
        return add

    def finish_row(ix, add):
        tiles = []
        for v in range(CM // 8):
            g, rv = (v // 3, v % 3) if v < 12 else (0, 3)
            s = w_s[ix, 8 * v : 8 * v + 8, :]
            if ix == 0:
                s = s + hx_s[0, 8 * v : 8 * v + 8, :]
            if ix == ROWS - 1:
                s = s + hx_s[1, 8 * v : 8 * v + 8, :]
            far = pltpu.roll(add[rv], (2 * LANES - (2 * ix + 1 + 32 * g)) % LANES, 1)
            other = jnp.where(
                lane % 4 == 3,
                pltpu.roll(s, LANES - 1, 1),
                jnp.where(lane % 4 == 0, pltpu.roll(s, 1, 1), F32(0.0)),
            )
            other = jnp.where((lane == 0) | (lane == LANES - 1), far, other)
            tiles.append(s + other)
        rate = F32(time_step) / tiles[12]
        q = r_s[pl.ds(ix, C, stride=ROWS), :]
        return q + jnp.concatenate([t * rate for t in tiles[:12]], axis=0)

    level = lax.broadcasted_iota(jnp.int32, (LEV, LANES), 0)

    def physics(j, new):
        vapour, heavy, deuter = new[:LEV], new[LEV : 2 * LEV], new[2 * LEV :]
        depth = F32(absorb_coef) * vapour
        for shift in (1, 2, 4, 8, 16):
            depth = depth + jnp.where(level >= shift, pltpu.roll(depth, shift, 0), F32(0.0))
        heating = F32(heat_gain * absorb_coef) * vapour * jnp.exp(-depth)
        warmed = tg_s[j] + jnp.where(dg_s[j][:1] == 1.0, heating, F32(0.0))
        saturation = F32(sat_base) * jnp.exp(F32(clausius) * (warmed - F32(ref_temp)))
        remain = jnp.minimum(vapour, saturation)
        log_ratio = jnp.log(remain / vapour)
        inverse = 1.0 / warmed
        alpha_heavy = jnp.exp(F32(1137.0) * inverse * inverse - F32(0.4156) * inverse - F32(0.0020667))
        alpha_deut = jnp.exp(F32(24844.0) * inverse * inverse - F32(76.248) * inverse + F32(0.052612))
        out = [remain, heavy * jnp.exp(alpha_heavy * log_ratio), deuter * jnp.exp(alpha_deut * log_ratio)]
        out = jnp.concatenate(out + [jnp.zeros((LEV, LANES), F32)], axis=0).T
        hi, lo = split(out)
        xt_s[LANES * j : LANES * (j + 1), :LANES] = hi
        xt_s[LANES * j : LANES * (j + 1), LANES:] = lo

    add = edge_lanes(False)
    for j, ix in enumerate(KEEP):
        physics(j, finish_row(ix, add))

    row8 = lax.broadcasted_iota(jnp.int32, (1, 8, LANES), 1)
    lane8 = lax.broadcasted_iota(jnp.int32, (1, 8, LANES), 2)
    top, late = row8 >= 2, lane8 >= C

    def send_copy(p, slot):
        return pltpu.make_async_remote_copy(
            s_s.at[p], rc_s.at[slot], ssem.at[p], rsem.at[slot], device_id=(f, p), device_id_type=MESH
        )

    def send(rows_of_z):
        lhs = [oh_s[pl.ds(pl.multiple_of(zz * 96, 96), 96), :] for zz in rows_of_z]
        y = mm(jnp.concatenate(lhs, axis=0), xt_s[...])
        y = (y[:, :LANES] + y[:, LANES:]).reshape(8, PEER, LANES)
        v0, v1, v2 = y[:, 0:8], y[:, 8:16], y[:, 16:24]
        a0, a1, a2 = pltpu.roll(v2, 96, 2), pltpu.roll(v2, 64, 2), pltpu.roll(v2, 32, 2)
        v0 = jnp.where(late, jnp.where(top, a0, pltpu.roll(a2, 6, 1)), v0)
        v1 = jnp.where(late, jnp.where(top, a1, pltpu.roll(a2, 4, 1)), v1)
        v2 = jnp.where(late, pltpu.roll(a2, 2, 1), v2)
        for h in range(2):
            rows = pl.ds(rows_of_z[h] * NX, NX)
            s_s[rows, 0:8, :] = v0[4 * h : 4 * h + 4]
            s_s[rows, 8:16, :] = v1[4 * h : 4 * h + 4]
            s_s[rows, 16:18, :] = v2[4 * h : 4 * h + 4, 0:2]
        for h in range(2):
            for xx in range(NX):
                p = rows_of_z[h] * NX + (x + xx) % NX

                @pl.when(p != b)
                def _():
                    send_copy(p, b).start()

    pl.semaphore_wait(round_sem.at[0], len(row_mates))
    send([(z + 3) % NZ, (z + NZ - 3) % NZ])
    pl.semaphore_wait(round_sem.at[2], len(row_mates))

    def far_first(n, carry):
        k = 6 - n - n // 3
        back = k - jnp.where(n < 2, 1, jnp.where(n == 2, 2, jnp.where(n == 3, 1, k)))
        send([(z + k) % NZ, (z + NZ - back) % NZ])
        return carry

    lax.fori_loop(0, 5, far_first, 0)
    rc_s[b] = s_s[b]

    for slot in (1, 3, 5, 6, 7):
        halo_wait(slot)
    add = edge_lanes(True)
    for ix in range(ROWS):
        nt_s[pl.ds(ix, C, stride=ROWS), :] = finish_row(ix, add)
    for n in range(8):
        halo_copy(n).wait_send()

    def arrive(i, carry):
        @pl.when(i != b)
        def _():
            send_copy(i, b).wait_send()
            send_copy(i, i).wait_recv()

        return carry

    lax.fori_loop(0, NB, arrive, 0)


def write_kernel(nt_s, rc_s, nt_hbm, ph_hbm, ph_s, sem):
    out_nt = pltpu.make_async_copy(nt_s, nt_hbm, sem.at[0])
    out_nt.start()
    row8 = lax.broadcasted_iota(jnp.int32, (1, 8, LANES), 1)
    lane8 = lax.broadcasted_iota(jnp.int32, (1, 8, LANES), 2)
    outs = []
    for g in range(3):
        grp = pl.ds(16 * g, 16)
        v0, v1 = rc_s[grp, 0:8, :], rc_s[grp, 8:16, :]
        v2 = jnp.concatenate([rc_s[grp, 16:18, :], jnp.zeros((16, 6, LANES), F32)], axis=1)
        a2 = jnp.where(
            row8 < 4, pltpu.roll(v0, 2, 1), jnp.where(row8 < 6, pltpu.roll(v1, 4, 1), pltpu.roll(v2, 6, 1))
        )
        tail = jnp.where(
            lane8 < 32, pltpu.roll(v0, 32, 2), jnp.where(lane8 < 64, pltpu.roll(v1, 64, 2), pltpu.roll(a2, 96, 2))
        )
        v2 = jnp.where(row8 >= 2, tail, v2)
        cols = jnp.concatenate([v0, v1, v2], axis=1).reshape(16 * PEER, LANES)
        part = pl.ds(384 * g, 384)
        ph_s[:, part] = cols.T[:C]
        outs.append(pltpu.make_async_copy(ph_s.at[:, part], ph_hbm.at[:, part], sem.at[1 + g]))
        outs[-1].start()
    for cp in [out_nt] + outs:
        cp.wait()


def on_device(isotope_ratios, advecting_velocity, metric_scaling, thermal_state, outgoing_site_order, daytime_indicator):
    hbm = pl.BlockSpec(memory_space=pltpu.HBM)
    vm = lambda *shape, dtype=F32: pltpu.VMEM(shape, dtype)
    moved = (vm(C * ROWS, LANES), vm(NB, MSG, LANES))
    new_tracers, arrived = pl.pallas_call(
        step_kernel,
        out_shape=moved,
        in_specs=[hbm] * 8,
        out_specs=(pl.BlockSpec(memory_space=pltpu.VMEM),) * 2,
        scratch_shapes=[
            vm(C * ROWS, LANES), vm(2 * LEV * ROWS, LANES), vm(ROWS, LANES), vm(LEV, SITES),
            vm(1, SITES, dtype=jnp.int32), vm(1, SITES, dtype=jnp.int32),
            vm(2 * LANES, 2 * LANES, dtype=BF16), vm(384, 512, dtype=BF16),
            vm(ROWS, CM, LANES), vm(LEV, LANES), vm(2, CM, LANES), vm(6, LEV, LANES),
            vm(12, LEV, LANES), vm(12, 8, LANES),
            vm(SITES, 12 * LANES, dtype=BF16), vm(12 * LANES, 2 * LANES, dtype=BF16),
            vm(NB, MSG, LANES),
            pltpu.SemaphoreType.DMA((8,)),
            pltpu.SemaphoreType.DMA((8,)), pltpu.SemaphoreType.DMA((8,)),
            pltpu.SemaphoreType.DMA((NB,)), pltpu.SemaphoreType.DMA((NB,)),
            pltpu.SemaphoreType.REGULAR((3,)),
        ],
        compiler_params=pltpu.CompilerParams(
            collective_id=0, has_side_effects=True, vmem_limit_bytes=GRANT - 1536 * 1024
        ),
        name="transport_condense",
    )(
        isotope_ratios.reshape(C * ROWS, LANES),
        advecting_velocity.reshape(2 * LEV * ROWS, LANES),
        metric_scaling,
        thermal_state[0],
        outgoing_site_order,
        daytime_indicator,
        jnp.asarray(lane_matrix()),
        jnp.asarray(expand_matrix()),
    )
    new_tracers, physics = pl.pallas_call(
        write_kernel,
        out_shape=(
            jax.ShapeDtypeStruct((C * ROWS, LANES), F32),
            jax.ShapeDtypeStruct((C, SITES), F32),
        ),
        in_specs=(pl.BlockSpec(memory_space=pltpu.VMEM),) * 2,
        out_specs=(hbm, hbm),
        scratch_shapes=[vm(C, SITES), pltpu.SemaphoreType.DMA((4,))],
        compiler_params=pltpu.CompilerParams(vmem_limit_bytes=8 * 1024 * 1024),
        name="write_results",
    )(new_tracers, arrived)
    return (new_tracers.reshape(3, LEV, ROWS, LANES), physics.reshape(1, 3, LEV, SITES))


def solution(mesh):
    placed = (
        P(None, None, "face", "blk"),
        P(None, None, "face", "blk"),
        P("face", "blk"),
        P("face", None, "blk"),
        P("face", "blk"),
        P("face", "blk"),
    )
    return jax.shard_map(
        on_device,
        mesh=mesh,
        in_specs=placed,
        out_specs=(P(None, None, "face", "blk"), P("face", None, None, "blk")),
        check_vma=False,
    )
```

```python
import functools
import math

import jax
import jax.numpy as jnp
import numpy as np
from jax import lax
from jax.experimental import pallas as pl
from jax.experimental.pallas import tpu as pltpu
from jax.sharding import PartitionSpec as P

time_step = 0.006
absorb_coef = 0.02
heat_gain = 100.0
sat_base = 3.0
clausius = 0.07
ref_temp = 280.0

MESH = pl.DeviceIdType.MESH
F32, BF16 = jnp.float32, jnp.bfloat16
NZ, NX = 12, 4
NB = NZ * NX
ROWS, LANES, LEV = 16, 128, 32
C = 3 * LEV
CM = C + 8
SITES, PEER = 1152, 24
MSG = 18
GRANT = 67043328
KEEP = [ix for ix in range(ROWS) if ix % 4 != 3]


def gll_tables():
    inv_root = 1.0 / math.sqrt(5.0)
    gll_nodes = np.array([-1.0, -inv_root, inv_root, 1.0])
    legendre = (5.0 * gll_nodes**3 - 3.0 * gll_nodes) / 2.0
    deriv_matrix = np.zeros((4, 4))
    for row_index in range(4):
        for col_index in range(4):
            if row_index != col_index:
                deriv_matrix[row_index, col_index] = legendre[row_index] / (
                    legendre[col_index] * (gll_nodes[row_index] - gll_nodes[col_index])
                )
    deriv_matrix[0, 0] = -3.0
    deriv_matrix[3, 3] = 3.0
    weights = np.array([1.0, 5.0, 5.0, 1.0]) / 6.0
    return (deriv_matrix, weights)


DERIV, WEIGHT = gll_tables()


def lane_matrix():
    kron = np.kron(np.eye(LANES // 4), (-WEIGHT[:, None] * DERIV)).T
    hi = kron.astype(jnp.bfloat16).astype(np.float32)
    lo = kron.astype(np.float32) - hi
    full = np.block([[hi, lo], [hi, np.zeros_like(lo)]])
    return full.astype(jnp.bfloat16)


def expand_matrix():
    out = np.zeros((384, 512), np.float32)
    for row in range(4):
        for lane in range(LANES):
            if lane % 4 != 3:
                out[96 * row + 3 * (lane // 4) + lane % 4, 128 * row + lane] = 1.0
    return out.astype(jnp.bfloat16)


def split(x):
    hi = x.astype(BF16)
    return hi, (x - hi.astype(F32)).astype(BF16)


def mm(a, b):
    return jnp.dot(a, b, preferred_element_type=F32)


def step_kernel(
    r_hbm, v_hbm, m_hbm, t_hbm, o_hbm, d_hbm, k_hbm, e_hbm,
    nt_s, rc_s,
    r_s, v_s, m_s, t_s, o_s, d_s, k_s, e_s,
    w_s, edge_s, hx_s, he_s, tg_s, dg_s, oh_s, xt_s, s_s, head_s, pack_s, turned_s,
    in_sem, hsend, hrecv, ssem, rsem, round_sem,
):
    f, b = lax.axis_index("face"), lax.axis_index("blk")
    nf = lax.axis_size("face")
    z, x = b // NX, b % NX
    fp, fn = (f + nf - 1) % nf, (f + 1) % nf
    bp, bn = (b + NB - 1) % NB, (b + 1) % NB

    loads = [
        pltpu.make_async_copy(src, dst, in_sem.at[i])
        for i, (src, dst) in enumerate(
            [(r_hbm, r_s), (v_hbm, v_s), (m_hbm, m_s), (k_hbm, k_s), (o_hbm, o_s), (t_hbm, t_s), (d_hbm, d_s), (e_hbm, e_s)]
        )
    ]
    for cp in loads:
        cp.start()

    halo = [(fp, b), (fn, b), (f, bp), (f, bn), (fp, bp), (fp, bn), (fn, bp), (fn, bn)]
    row_mates = [(f, z * NX + (x + d) % NX) for d in range(1, NX)]
    column_mates = [(f, (z + d) % NZ * NX + x) for d in (1, NZ - 1, 2, NZ - 2, 3, NZ - 3)]

    def greet(sem, peers):
        for peer in peers:
            pl.semaphore_signal(sem, inc=1, device_id=peer, device_id_type=MESH)

    barrier = pltpu.get_barrier_semaphore()
    near = column_mates[::-1] + halo + row_mates
    greet(barrier, near)

    lane = lax.broadcasted_iota(jnp.int32, (8, LANES), 1)
    wy = jnp.where((lane % 4 == 0) | (lane % 4 == 3), F32(WEIGHT[0]), F32(WEIGHT[1]))
    for cp in loads[:4]:
        cp.wait()

    for e in range(ROWS // 4):
        fx, fy = [], []
        for i in range(4):
            ix = 4 * e + i
            q = r_s[pl.ds(ix, C, stride=ROWS), :].reshape(3, LEV, LANES)
            met = m_s[ix : ix + 1, :]
            ax = v_s[pl.ds(ix, LEV, stride=ROWS), :] * met
            ay = v_s[pl.ds(LEV * ROWS + ix, LEV, stride=ROWS), :] * met
            fx.append((ax[None] * q).reshape(C, LANES))
            fy.append((ay[None] * q).reshape(C, LANES))
        hi, lo = split(jnp.concatenate(fy, axis=0))
        gy = mm(jnp.concatenate([hi, lo], axis=1), k_s[...])
        gy = gy[:, :LANES] + gy[:, LANES:]
        for i in range(4):
            gx = None
            for j in range(4):
                if DERIV[i, j] != 0.0:
                    term = F32(-WEIGHT[i] * DERIV[i, j]) * fx[j]
                    gx = term if gx is None else gx + term
            w_s[4 * e + i, :C, :] = F32(WEIGHT[i]) * gy[C * i : C * (i + 1)] + wy[:1] * gx
            w_s[4 * e + i, C:, :] = F32(WEIGHT[i]) * wy * m_s[4 * e + i : 4 * e + i + 1, :]

    for e in range(1, ROWS // 4):
        both = w_s[4 * e - 1] + w_s[4 * e]
        w_s[4 * e - 1] = both
        w_s[4 * e] = both
    edge = [jnp.zeros((8, LANES), F32) for _ in range(4)]
    for ix in range(ROWS):
        for v in range(CM // 8):
            g, rv = (v // 3, v % 3) if v < 12 else (0, 3)
            tile = w_s[ix, 8 * v : 8 * v + 8, :]
            moved = pltpu.roll(tile, (1 + 2 * ix + 32 * g) % LANES, 1)
            edge[rv] = jnp.where(lane // 2 == ix + 16 * g, moved, edge[rv])
    for rv in range(4):
        edge_s[8 * rv : 8 * rv + 8, :] = edge[rv]

    pl.semaphore_wait(barrier, len(near))
    greet(round_sem.at[1], column_mates[4:])
    greet(round_sem.at[0], row_mates)

    def halo_copy(n):
        src = w_s.at[0] if n == 0 else w_s.at[ROWS - 1] if n == 1 else edge_s
        slot = [1, 0, 3, 2, 7, 6, 5, 4][n]
        dst = hx_s.at[slot] if n < 2 else he_s.at[slot - 2]
        return pltpu.make_async_remote_copy(
            src, dst, hsend.at[n], hrecv.at[slot], device_id=halo[n], device_id_type=MESH
        )

    def halo_wait(slot):
        dst = hx_s.at[slot] if slot < 2 else he_s.at[slot - 2]
        pltpu.make_async_remote_copy(
            dst, dst, hsend.at[slot], hrecv.at[slot], device_id=halo[slot], device_id_type=MESH
        ).wait_recv()

    for n in (7, 1, 3, 6, 5, 4, 0, 2):
        halo_copy(n).start()

    for cp in loads[4:]:
        cp.wait()
    warm = [t_s[:, 384 * k : 384 * k + 384] - F32(ref_temp) for k in range(3)]
    warm = jnp.concatenate(warm, axis=0)
    w_hi, w_lo = split(warm)
    w_lo2 = (warm - w_hi.astype(F32) - w_lo.astype(F32)).astype(BF16)
    day = [jnp.broadcast_to(d_s[:, 384 * k : 384 * k + 384].astype(F32), (16, 384)) for k in range(3)]
    day = jnp.concatenate(day, axis=0).astype(BF16)
    grid = mm(jnp.concatenate([w_hi, w_lo, w_lo2, day], axis=0), e_s[...])
    heat = grid[:C] + grid[C : 2 * C] + grid[2 * C : 3 * C] + F32(ref_temp)
    for k in range(3):
        for i in range(4):
            tg_s[4 * k + i] = heat[LEV * k : LEV * (k + 1), LANES * i : LANES * (i + 1)]
            dg_s[4 * k + i] = grid[3 * C + 16 * k : 3 * C + 16 * k + 8, LANES * i : LANES * (i + 1)]

    site = jnp.where(lane % 4 == 3, -4096, 3 * (lane // 4) + lane % 4)[:1]
    for k in range(SITES // LANES):
        want = jnp.broadcast_to(o_s[:, LANES * k : LANES * (k + 1)], (LANES, LANES)).T
        for j in range(12):
            oh_s[LANES * k : LANES * (k + 1), LANES * j : LANES * (j + 1)] = jnp.where(
                want == site + 96 * j, F32(1.0), F32(0.0)
            ).astype(BF16)


    pos = lane % 32

    def edge_lanes(whole):
        add = []
        for rv in range(4):
            rows = pl.ds(8 * rv, 8)
            before = pltpu.roll(he_s[0, rows, :], 1, 1)
            before = before + jnp.where(pos == 1, pltpu.roll(he_s[2, rows, :], LANES - 29, 1), F32(0.0))
            after = jnp.zeros_like(before)
            if whole:
                after = pltpu.roll(he_s[1, rows, :], LANES - 1, 1)
                before = before + jnp.where(pos == 31, pltpu.roll(he_s[4, rows, :], 31, 1), F32(0.0))
                after = after + jnp.where(pos == 0, pltpu.roll(he_s[3, rows, :], LANES - 31, 1), F32(0.0))
                after = after + jnp.where(pos == 30, pltpu.roll(he_s[5, rows, :], 29, 1), F32(0.0))
            add.append(jnp.where(pos % 2 == 1, before, after))
        return add

    def finish_row(ix, add):
        tiles = []
        for v in range(CM // 8):
            g, rv = (v // 3, v % 3) if v < 12 else (0, 3)
            s = w_s[ix, 8 * v : 8 * v + 8, :]
            if ix == 0:
                s = s + hx_s[0, 8 * v : 8 * v + 8, :]
            if ix == ROWS - 1:
                s = s + hx_s[1, 8 * v : 8 * v + 8, :]
            far = F32(0.0)
            if add is not None:
                far = pltpu.roll(add[rv], (2 * LANES - (2 * ix + 1 + 32 * g)) % LANES, 1)
            other = jnp.where(
                lane % 4 == 3,
                pltpu.roll(s, LANES - 1, 1),
                jnp.where(lane % 4 == 0, pltpu.roll(s, 1, 1), F32(0.0)),
            )
            other = jnp.where((lane == 0) | (lane == LANES - 1), far, other)
            tiles.append(s + other)
        rate = F32(time_step) / tiles[12]
        q = r_s[pl.ds(ix, C, stride=ROWS), :]
        return q + jnp.concatenate([t * rate for t in tiles[:12]], axis=0)

    level = lax.broadcasted_iota(jnp.int32, (LEV, LANES), 0)

    def physics(new, warmth, day):
        vapour, heavy, deuter = new[:LEV], new[LEV : 2 * LEV], new[2 * LEV :]
        depth = F32(absorb_coef) * vapour
        for shift in (1, 2, 4, 8, 16):
            depth = depth + jnp.where(level >= shift, pltpu.roll(depth, shift, 0), F32(0.0))
        heating = F32(heat_gain * absorb_coef) * vapour * jnp.exp(-depth)
        warmed = warmth + jnp.where(day == 1.0, heating, F32(0.0))
        saturation = F32(sat_base) * jnp.exp(F32(clausius) * (warmed - F32(ref_temp)))
        remain = jnp.minimum(vapour, saturation)
        log_ratio = jnp.log(remain / vapour)
        inverse = 1.0 / warmed
        alpha_heavy = jnp.exp(F32(1137.0) * inverse * inverse - F32(0.4156) * inverse - F32(0.0020667))
        alpha_deut = jnp.exp(F32(24844.0) * inverse * inverse - F32(76.248) * inverse + F32(0.052612))
        out = [remain, heavy * jnp.exp(alpha_heavy * log_ratio), deuter * jnp.exp(alpha_deut * log_ratio)]
        return jnp.concatenate(out + [jnp.zeros((LEV, LANES), F32)], axis=0).T

    def put(row, values):
        hi, lo = split(values)
        xt_s[row : row + values.shape[0], :LANES] = hi
        xt_s[row : row + values.shape[0], LANES:] = lo

    wide = lax.broadcasted_iota(jnp.int32, (1, LANES), 1)
    ratio0 = jnp.full((C, LANES), F32(1.0))
    warm0 = jnp.full((LEV, LANES), F32(ref_temp))
    day0 = jnp.zeros((8, LANES), F32)
    for j, ix in enumerate(KEEP):
        if ix == 0:
            continue
        out = physics(finish_row(ix, None), tg_s[j], dg_s[j][:1])
        put(LANES * j, out)
        head_s[j] = out[:16]
        here = wide == 2 * ix + 1
        ratio0 = jnp.where(here, pltpu.roll(r_s[pl.ds(ix, C, stride=ROWS), :], 2 * ix + 1, 1), ratio0)
        warm0 = jnp.where(here, pltpu.roll(tg_s[j], 2 * ix + 1, 1), warm0)
        day0 = jnp.where(here, pltpu.roll(dg_s[j], 2 * ix + 1, 1), day0)
    pack_s[:C] = ratio0
    pack_s[C : C + LEV] = warm0
    pack_s[C + LEV :] = day0

    pl.semaphore_wait(round_sem.at[1], 2)
    greet(round_sem.at[2], row_mates)
    for slot in (0, 2, 4):
        halo_wait(slot)
    add = edge_lanes(False)
    put(0, physics(finish_row(0, add), tg_s[0], dg_s[0][:1]))
    sums = [edge_s[8 * rv : 8 * rv + 8, :] + add[rv] for rv in range(4)]
    rate = F32(time_step) / jnp.where((wide < 32) & (wide % 2 == 1), sums[3], F32(1.0))
    lanes0 = [
        pack_s[8 * v : 8 * v + 8] + rate * pltpu.roll(sums[v % 3], (LANES - 32 * (v // 3)) % LANES, 1)
        for v in range(C // 8)
    ]
    turned_s[...] = physics(jnp.concatenate(lanes0, axis=0), pack_s[C : C + LEV], pack_s[C + LEV : C + LEV + 1])
    first = lax.broadcasted_iota(jnp.int32, (16, LANES), 0) == 0
    for j, ix in enumerate(KEEP):
        if ix != 0:
            put(LANES * j, jnp.where(first, turned_s[2 * ix + 1 : 2 * ix + 2, :], head_s[j]))

    row8 = lax.broadcasted_iota(jnp.int32, (1, 8, LANES), 1)
    lane8 = lax.broadcasted_iota(jnp.int32, (1, 8, LANES), 2)
    top, late = row8 >= 2, lane8 >= C

    def send_copy(p, slot):
        return pltpu.make_async_remote_copy(
            s_s.at[p], rc_s.at[slot], ssem.at[0], rsem.at[0], device_id=(f, p), device_id_type=MESH
        )

    def send(rows_of_z):
        lhs = [oh_s[pl.ds(pl.multiple_of(zz * 96, 96), 96), :] for zz in rows_of_z]
        y = mm(jnp.concatenate(lhs, axis=0), xt_s[...])
        y = (y[:, :LANES] + y[:, LANES:]).reshape(8, PEER, LANES)
        v0, v1, v2 = y[:, 0:8], y[:, 8:16], y[:, 16:24]
        a0, a1, a2 = pltpu.roll(v2, 96, 2), pltpu.roll(v2, 64, 2), pltpu.roll(v2, 32, 2)
        v0 = jnp.where(late, jnp.where(top, a0, pltpu.roll(a2, 6, 1)), v0)
        v1 = jnp.where(late, jnp.where(top, a1, pltpu.roll(a2, 4, 1)), v1)
        v2 = jnp.where(late, pltpu.roll(a2, 2, 1), v2)
        for h in range(2):
            rows = pl.ds(rows_of_z[h] * NX, NX)
            s_s[rows, 0:8, :] = v0[4 * h : 4 * h + 4]
            s_s[rows, 8:16, :] = v1[4 * h : 4 * h + 4]
            s_s[rows, 16:18, :] = v2[4 * h : 4 * h + 4, 0:2]
        for h in range(2):
            for xx in range(NX):
                p = rows_of_z[h] * NX + (x + xx) % NX

                @pl.when(p != b)
                def _():
                    send_copy(p, b).start()

    pl.semaphore_wait(round_sem.at[0], len(row_mates))
    send([(z + 3) % NZ, (z + NZ - 3) % NZ])
    pl.semaphore_wait(round_sem.at[2], len(row_mates))

    def far_first(n, carry):
        k = 6 - n - n // 3
        back = k - jnp.where(n < 2, 1, jnp.where(n == 2, 2, jnp.where(n == 3, 1, k)))
        send([(z + k) % NZ, (z + NZ - back) % NZ])
        return carry

    lax.fori_loop(0, 5, far_first, 0)
    rc_s[b] = s_s[b]

    for slot in (1, 3, 5, 6, 7):
        halo_wait(slot)
    add = edge_lanes(True)
    for ix in range(ROWS):
        nt_s[pl.ds(ix, C, stride=ROWS), :] = finish_row(ix, add)
    for n in range(8):
        halo_copy(n).wait_send()

    others = pl.ds(0, NB - 1)
    pltpu.make_async_remote_copy(
        s_s.at[others], rc_s.at[others], ssem.at[0], rsem.at[0], device_id=(f, bn), device_id_type=MESH
    ).wait()


def write_kernel(nt_s, rc_s, nt_hbm, ph_hbm, ph_s, sem):
    out_nt = pltpu.make_async_copy(nt_s, nt_hbm, sem.at[0])
    out_nt.start()
    row8 = lax.broadcasted_iota(jnp.int32, (1, 8, LANES), 1)
    lane8 = lax.broadcasted_iota(jnp.int32, (1, 8, LANES), 2)
    outs = []
    for g in range(3):
        grp = pl.ds(16 * g, 16)
        v0, v1 = rc_s[grp, 0:8, :], rc_s[grp, 8:16, :]
        v2 = jnp.concatenate([rc_s[grp, 16:18, :], jnp.zeros((16, 6, LANES), F32)], axis=1)
        a2 = jnp.where(
            row8 < 4, pltpu.roll(v0, 2, 1), jnp.where(row8 < 6, pltpu.roll(v1, 4, 1), pltpu.roll(v2, 6, 1))
        )
        tail = jnp.where(
            lane8 < 32, pltpu.roll(v0, 32, 2), jnp.where(lane8 < 64, pltpu.roll(v1, 64, 2), pltpu.roll(a2, 96, 2))
        )
        v2 = jnp.where(row8 >= 2, tail, v2)
        cols = jnp.concatenate([v0, v1, v2], axis=1).reshape(16 * PEER, LANES)
        part = pl.ds(384 * g, 384)
        ph_s[:, part] = cols.T[:C]
        outs.append(pltpu.make_async_copy(ph_s.at[:, part], ph_hbm.at[:, part], sem.at[1 + g]))
        outs[-1].start()
    for cp in [out_nt] + outs:
        cp.wait()


def on_device(isotope_ratios, advecting_velocity, metric_scaling, thermal_state, outgoing_site_order, daytime_indicator):
    hbm = pl.BlockSpec(memory_space=pltpu.HBM)
    vm = lambda *shape, dtype=F32: pltpu.VMEM(shape, dtype)
    moved = (vm(C * ROWS, LANES), vm(NB, MSG, LANES))
    new_tracers, arrived = pl.pallas_call(
        step_kernel,
        out_shape=moved,
        in_specs=[hbm] * 8,
        out_specs=(pl.BlockSpec(memory_space=pltpu.VMEM),) * 2,
        scratch_shapes=[
            vm(C * ROWS, LANES), vm(2 * LEV * ROWS, LANES), vm(ROWS, LANES), vm(LEV, SITES),
            vm(1, SITES, dtype=jnp.int32), vm(1, SITES, dtype=jnp.int32),
            vm(2 * LANES, 2 * LANES, dtype=BF16), vm(384, 512, dtype=BF16),
            vm(ROWS, CM, LANES), vm(LEV, LANES), vm(2, CM, LANES), vm(6, LEV, LANES),
            vm(12, LEV, LANES), vm(12, 8, LANES),
            vm(SITES, 12 * LANES, dtype=BF16), vm(12 * LANES, 2 * LANES, dtype=BF16),
            vm(NB, MSG, LANES),
            vm(12, 16, LANES), vm(C + LEV + 8, LANES), vm(LANES, LANES),
            pltpu.SemaphoreType.DMA((8,)),
            pltpu.SemaphoreType.DMA((8,)), pltpu.SemaphoreType.DMA((8,)),
            pltpu.SemaphoreType.DMA((1,)), pltpu.SemaphoreType.DMA((1,)),
            pltpu.SemaphoreType.REGULAR((3,)),
        ],
        compiler_params=pltpu.CompilerParams(
            collective_id=0, has_side_effects=True, vmem_limit_bytes=GRANT - 1536 * 1024
        ),
        name="transport_condense",
    )(
        isotope_ratios.reshape(C * ROWS, LANES),
        advecting_velocity.reshape(2 * LEV * ROWS, LANES),
        metric_scaling,
        thermal_state[0],
        outgoing_site_order,
        daytime_indicator,
        jnp.asarray(lane_matrix()),
        jnp.asarray(expand_matrix()),
    )
    new_tracers, physics = pl.pallas_call(
        write_kernel,
        out_shape=(
            jax.ShapeDtypeStruct((C * ROWS, LANES), F32),
            jax.ShapeDtypeStruct((C, SITES), F32),
        ),
        in_specs=(pl.BlockSpec(memory_space=pltpu.VMEM),) * 2,
        out_specs=(hbm, hbm),
        scratch_shapes=[vm(C, SITES), pltpu.SemaphoreType.DMA((4,))],
        compiler_params=pltpu.CompilerParams(vmem_limit_bytes=8 * 1024 * 1024),
        name="write_results",
    )(new_tracers, arrived)
    return (new_tracers.reshape(3, LEV, ROWS, LANES), physics.reshape(1, 3, LEV, SITES))


def solution(mesh):
    placed = (
        P(None, None, "face", "blk"),
        P(None, None, "face", "blk"),
        P("face", "blk"),
        P("face", None, "blk"),
        P("face", "blk"),
        P("face", "blk"),
    )
    return jax.shard_map(
        on_device,
        mesh=mesh,
        in_specs=placed,
        out_specs=(P(None, None, "face", "blk"), P("face", None, None, "blk")),
        check_vma=False,
    )
```

```python
import functools
import math

import jax
import jax.numpy as jnp
import numpy as np
from jax import lax
from jax.experimental import pallas as pl
from jax.experimental.pallas import tpu as pltpu
from jax.sharding import PartitionSpec as P

time_step = 0.006
absorb_coef = 0.02
heat_gain = 100.0
sat_base = 3.0
clausius = 0.07
ref_temp = 280.0

MESH = pl.DeviceIdType.MESH
F32, BF16 = jnp.float32, jnp.bfloat16
NZ, NX = 12, 4
NB = NZ * NX
ROWS, LANES, LEV = 16, 128, 32
C = 3 * LEV
CM = C + 8
SITES, PEER = 1152, 24
MSG = 18
GRANT = 67043328
KEEP = [ix for ix in range(ROWS) if ix % 4 != 3]


def gll_tables():
    inv_root = 1.0 / math.sqrt(5.0)
    gll_nodes = np.array([-1.0, -inv_root, inv_root, 1.0])
    legendre = (5.0 * gll_nodes**3 - 3.0 * gll_nodes) / 2.0
    deriv_matrix = np.zeros((4, 4))
    for row_index in range(4):
        for col_index in range(4):
            if row_index != col_index:
                deriv_matrix[row_index, col_index] = legendre[row_index] / (
                    legendre[col_index] * (gll_nodes[row_index] - gll_nodes[col_index])
                )
    deriv_matrix[0, 0] = -3.0
    deriv_matrix[3, 3] = 3.0
    weights = np.array([1.0, 5.0, 5.0, 1.0]) / 6.0
    return (deriv_matrix, weights)


DERIV, WEIGHT = gll_tables()


def lane_matrix():
    kron = np.kron(np.eye(LANES // 4), (-WEIGHT[:, None] * DERIV)).T
    hi = kron.astype(jnp.bfloat16).astype(np.float32)
    lo = kron.astype(np.float32) - hi
    full = np.block([[hi, lo], [hi, np.zeros_like(lo)]])
    return full.astype(jnp.bfloat16)


def expand_matrix():
    out = np.zeros((384, 512), np.float32)
    for row in range(4):
        for lane in range(LANES):
            if lane % 4 != 3:
                out[96 * row + 3 * (lane // 4) + lane % 4, 128 * row + lane] = 1.0
    return out.astype(jnp.bfloat16)


def split(x):
    hi = x.astype(BF16)
    return hi, (x - hi.astype(F32)).astype(BF16)


def mm(a, b):
    return jnp.dot(a, b, preferred_element_type=F32)


def step_kernel(
    r_hbm, v_hbm, m_hbm, t_hbm, o_hbm, d_hbm, k_hbm, e_hbm,
    nt_s, rc_s,
    r_s, v_s, m_s, t_s, o_s, d_s, k_s, e_s,
    w_s, edge_s, hx_s, he_s, tg_s, dg_s, oh_s, xt_s, s_s, head_s, pack_s, turned_s,
    in_sem, hsend, hrecv, ssem, rsem, round_sem,
):
    f, b = lax.axis_index("face"), lax.axis_index("blk")
    nf = lax.axis_size("face")
    z, x = b // NX, b % NX
    fp, fn = (f + nf - 1) % nf, (f + 1) % nf
    bp, bn = (b + NB - 1) % NB, (b + 1) % NB

    loads = [
        pltpu.make_async_copy(src, dst, in_sem.at[i])
        for i, (src, dst) in enumerate(
            [(r_hbm, r_s), (v_hbm, v_s), (m_hbm, m_s), (k_hbm, k_s), (o_hbm, o_s), (t_hbm, t_s), (d_hbm, d_s), (e_hbm, e_s)]
        )
    ]
    for cp in loads:
        cp.start()

    halo = [(fp, b), (fn, b), (f, bp), (f, bn), (fp, bp), (fp, bn), (fn, bp), (fn, bn)]
    row_mates = [(f, z * NX + (x + d) % NX) for d in range(1, NX)]
    column_mates = [(f, (z + d) % NZ * NX + x) for d in (1, NZ - 1, 2, NZ - 2, 3, NZ - 3)]

    def greet(sem, peers):
        for peer in peers:
            pl.semaphore_signal(sem, inc=1, device_id=peer, device_id_type=MESH)

    barrier = pltpu.get_barrier_semaphore()
    near = column_mates[::-1] + halo + row_mates
    greet(barrier, near)

    lane = lax.broadcasted_iota(jnp.int32, (8, LANES), 1)
    wy = jnp.where((lane % 4 == 0) | (lane % 4 == 3), F32(WEIGHT[0]), F32(WEIGHT[1]))
    for cp in loads[:4]:
        cp.wait()

    for e in range(ROWS // 4):
        fx, fy = [], []
        for i in range(4):
            ix = 4 * e + i
            q = r_s[pl.ds(ix, C, stride=ROWS), :].reshape(3, LEV, LANES)
            met = m_s[ix : ix + 1, :]
            ax = v_s[pl.ds(ix, LEV, stride=ROWS), :] * met
            ay = v_s[pl.ds(LEV * ROWS + ix, LEV, stride=ROWS), :] * met
            fx.append((ax[None] * q).reshape(C, LANES))
            fy.append((ay[None] * q).reshape(C, LANES))
        hi, lo = split(jnp.concatenate(fy, axis=0))
        gy = mm(jnp.concatenate([hi, lo], axis=1), k_s[...])
        gy = gy[:, :LANES] + gy[:, LANES:]
        for i in range(4):
            gx = None
            for j in range(4):
                if DERIV[i, j] != 0.0:
                    term = F32(-WEIGHT[i] * DERIV[i, j]) * fx[j]
                    gx = term if gx is None else gx + term
            w_s[4 * e + i, :C, :] = F32(WEIGHT[i]) * gy[C * i : C * (i + 1)] + wy[:1] * gx
            w_s[4 * e + i, C:, :] = F32(WEIGHT[i]) * wy * m_s[4 * e + i : 4 * e + i + 1, :]

    for e in range(1, ROWS // 4):
        both = w_s[4 * e - 1] + w_s[4 * e]
        w_s[4 * e - 1] = both
        w_s[4 * e] = both
    edge = [jnp.zeros((8, LANES), F32) for _ in range(4)]
    for ix in range(ROWS):
        for v in range(CM // 8):
            g, rv = (v // 3, v % 3) if v < 12 else (0, 3)
            tile = w_s[ix, 8 * v : 8 * v + 8, :]
            moved = pltpu.roll(tile, (1 + 2 * ix + 32 * g) % LANES, 1)
            edge[rv] = jnp.where(lane // 2 == ix + 16 * g, moved, edge[rv])
    for rv in range(4):
        edge_s[8 * rv : 8 * rv + 8, :] = edge[rv]

    pl.semaphore_wait(barrier, len(near))
    greet(round_sem.at[0], column_mates[4:])

    def halo_copy(n):
        src = w_s.at[0] if n == 0 else w_s.at[ROWS - 1] if n == 1 else edge_s
        slot = [1, 0, 3, 2, 7, 6, 5, 4][n]
        dst = hx_s.at[slot] if n < 2 else he_s.at[slot - 2]
        return pltpu.make_async_remote_copy(
            src, dst, hsend.at[n], hrecv.at[slot], device_id=halo[n], device_id_type=MESH
        )

    def halo_wait(slot):
        dst = hx_s.at[slot] if slot < 2 else he_s.at[slot - 2]
        pltpu.make_async_remote_copy(
            dst, dst, hsend.at[slot], hrecv.at[slot], device_id=halo[slot], device_id_type=MESH
        ).wait_recv()

    for n in (7, 1, 3, 6, 5, 4, 0, 2):
        halo_copy(n).start()

    for cp in loads[4:]:
        cp.wait()
    warm = [t_s[:, 384 * k : 384 * k + 384] - F32(ref_temp) for k in range(3)]
    warm = jnp.concatenate(warm, axis=0)
    w_hi, w_lo = split(warm)
    w_lo2 = (warm - w_hi.astype(F32) - w_lo.astype(F32)).astype(BF16)
    day = [jnp.broadcast_to(d_s[:, 384 * k : 384 * k + 384].astype(F32), (16, 384)) for k in range(3)]
    day = jnp.concatenate(day, axis=0).astype(BF16)
    grid = mm(jnp.concatenate([w_hi, w_lo, w_lo2, day], axis=0), e_s[...])
    heat = grid[:C] + grid[C : 2 * C] + grid[2 * C : 3 * C] + F32(ref_temp)
    for k in range(3):
        for i in range(4):
            tg_s[4 * k + i] = heat[LEV * k : LEV * (k + 1), LANES * i : LANES * (i + 1)]
            dg_s[4 * k + i] = grid[3 * C + 16 * k : 3 * C + 16 * k + 8, LANES * i : LANES * (i + 1)]

    site = jnp.where(lane % 4 == 3, -4096, 3 * (lane // 4) + lane % 4)[:1]
    for k in range(SITES // LANES):
        want = jnp.broadcast_to(o_s[:, LANES * k : LANES * (k + 1)], (LANES, LANES)).T
        for j in range(12):
            oh_s[LANES * k : LANES * (k + 1), LANES * j : LANES * (j + 1)] = jnp.where(
                want == site + 96 * j, F32(1.0), F32(0.0)
            ).astype(BF16)


    pos = lane % 32

    def edge_lanes(whole):
        add = []
        for rv in range(4):
            rows = pl.ds(8 * rv, 8)
            before = pltpu.roll(he_s[0, rows, :], 1, 1)
            before = before + jnp.where(pos == 1, pltpu.roll(he_s[2, rows, :], LANES - 29, 1), F32(0.0))
            after = jnp.zeros_like(before)
            if whole:
                after = pltpu.roll(he_s[1, rows, :], LANES - 1, 1)
                before = before + jnp.where(pos == 31, pltpu.roll(he_s[4, rows, :], 31, 1), F32(0.0))
                after = after + jnp.where(pos == 0, pltpu.roll(he_s[3, rows, :], LANES - 31, 1), F32(0.0))
                after = after + jnp.where(pos == 30, pltpu.roll(he_s[5, rows, :], 29, 1), F32(0.0))
            add.append(jnp.where(pos % 2 == 1, before, after))
        return add

    def finish_row(ix, add):
        tiles = []
        for v in range(CM // 8):
            g, rv = (v // 3, v % 3) if v < 12 else (0, 3)
            s = w_s[ix, 8 * v : 8 * v + 8, :]
            if ix == 0:
                s = s + hx_s[0, 8 * v : 8 * v + 8, :]
            if ix == ROWS - 1:
                s = s + hx_s[1, 8 * v : 8 * v + 8, :]
            far = F32(0.0)
            if add is not None:
                far = pltpu.roll(add[rv], (2 * LANES - (2 * ix + 1 + 32 * g)) % LANES, 1)
            other = jnp.where(
                lane % 4 == 3,
                pltpu.roll(s, LANES - 1, 1),
                jnp.where(lane % 4 == 0, pltpu.roll(s, 1, 1), F32(0.0)),
            )
            other = jnp.where((lane == 0) | (lane == LANES - 1), far, other)
            tiles.append(s + other)
        rate = F32(time_step) / tiles[12]
        q = r_s[pl.ds(ix, C, stride=ROWS), :]
        return q + jnp.concatenate([t * rate for t in tiles[:12]], axis=0)

    level = lax.broadcasted_iota(jnp.int32, (LEV, LANES), 0)

    def physics(new, warmth, day):
        vapour, heavy, deuter = new[:LEV], new[LEV : 2 * LEV], new[2 * LEV :]
        depth = F32(absorb_coef) * vapour
        for shift in (1, 2, 4, 8, 16):
            depth = depth + jnp.where(level >= shift, pltpu.roll(depth, shift, 0), F32(0.0))
        heating = F32(heat_gain * absorb_coef) * vapour * jnp.exp(-depth)
        warmed = warmth + jnp.where(day == 1.0, heating, F32(0.0))
        saturation = F32(sat_base) * jnp.exp(F32(clausius) * (warmed - F32(ref_temp)))
        remain = jnp.minimum(vapour, saturation)
        log_ratio = jnp.log(remain / vapour)
        inverse = 1.0 / warmed
        alpha_heavy = jnp.exp(F32(1137.0) * inverse * inverse - F32(0.4156) * inverse - F32(0.0020667))
        alpha_deut = jnp.exp(F32(24844.0) * inverse * inverse - F32(76.248) * inverse + F32(0.052612))
        out = [remain, heavy * jnp.exp(alpha_heavy * log_ratio), deuter * jnp.exp(alpha_deut * log_ratio)]
        return jnp.concatenate(out + [jnp.zeros((LEV, LANES), F32)], axis=0).T

    def put(row, values):
        hi, lo = split(values)
        xt_s[row : row + values.shape[0], :LANES] = hi
        xt_s[row : row + values.shape[0], LANES:] = lo

    wide = lax.broadcasted_iota(jnp.int32, (1, LANES), 1)
    ratio0 = jnp.full((C, LANES), F32(1.0))
    warm0 = jnp.full((LEV, LANES), F32(ref_temp))
    day0 = jnp.zeros((8, LANES), F32)
    for j, ix in enumerate(KEEP):
        if ix == 0:
            continue
        out = physics(finish_row(ix, None), tg_s[j], dg_s[j][:1])
        put(LANES * j, out)
        head_s[j] = out[:16]
        here = wide == 2 * ix + 1
        ratio0 = jnp.where(here, pltpu.roll(r_s[pl.ds(ix, C, stride=ROWS), :], 2 * ix + 1, 1), ratio0)
        warm0 = jnp.where(here, pltpu.roll(tg_s[j], 2 * ix + 1, 1), warm0)
        day0 = jnp.where(here, pltpu.roll(dg_s[j], 2 * ix + 1, 1), day0)
    pack_s[:C] = ratio0
    pack_s[C : C + LEV] = warm0
    pack_s[C + LEV :] = day0

    pl.semaphore_wait(round_sem.at[0], 2)
    greet(round_sem.at[1], row_mates)
    for slot in (0, 2, 4):
        halo_wait(slot)
    add = edge_lanes(False)
    put(0, physics(finish_row(0, add), tg_s[0], dg_s[0][:1]))
    sums = [edge_s[8 * rv : 8 * rv + 8, :] + add[rv] for rv in range(4)]
    rate = F32(time_step) / jnp.where((wide < 32) & (wide % 2 == 1), sums[3], F32(1.0))
    lanes0 = [
        pack_s[8 * v : 8 * v + 8] + rate * pltpu.roll(sums[v % 3], (LANES - 32 * (v // 3)) % LANES, 1)
        for v in range(C // 8)
    ]
    turned_s[...] = physics(jnp.concatenate(lanes0, axis=0), pack_s[C : C + LEV], pack_s[C + LEV : C + LEV + 1])
    first = lax.broadcasted_iota(jnp.int32, (16, LANES), 0) == 0
    for j, ix in enumerate(KEEP):
        if ix != 0:
            put(LANES * j, jnp.where(first, turned_s[2 * ix + 1 : 2 * ix + 2, :], head_s[j]))

    row8 = lax.broadcasted_iota(jnp.int32, (1, 8, LANES), 1)
    lane8 = lax.broadcasted_iota(jnp.int32, (1, 8, LANES), 2)
    top, late = row8 >= 2, lane8 >= C

    def send_copy(p, slot):
        return pltpu.make_async_remote_copy(
            s_s.at[p], rc_s.at[slot], ssem.at[0], rsem.at[0], device_id=(f, p), device_id_type=MESH
        )

    def send(rows_of_z):
        lhs = [oh_s[pl.ds(pl.multiple_of(zz * 96, 96), 96), :] for zz in rows_of_z]
        y = mm(jnp.concatenate(lhs, axis=0), xt_s[...])
        y = (y[:, :LANES] + y[:, LANES:]).reshape(8, PEER, LANES)
        v0, v1, v2 = y[:, 0:8], y[:, 8:16], y[:, 16:24]
        a0, a1, a2 = pltpu.roll(v2, 96, 2), pltpu.roll(v2, 64, 2), pltpu.roll(v2, 32, 2)
        v0 = jnp.where(late, jnp.where(top, a0, pltpu.roll(a2, 6, 1)), v0)
        v1 = jnp.where(late, jnp.where(top, a1, pltpu.roll(a2, 4, 1)), v1)
        v2 = jnp.where(late, pltpu.roll(a2, 2, 1), v2)
        for h in range(2):
            rows = pl.ds(rows_of_z[h] * NX, NX)
            s_s[rows, 0:8, :] = v0[4 * h : 4 * h + 4]
            s_s[rows, 8:16, :] = v1[4 * h : 4 * h + 4]
            s_s[rows, 16:18, :] = v2[4 * h : 4 * h + 4, 0:2]
        for h in range(2):
            for xx in range(NX):
                p = rows_of_z[h] * NX + (x + xx) % NX

                @pl.when(p != b)
                def _():
                    send_copy(p, b).start()

    pl.semaphore_wait(round_sem.at[1], len(row_mates))

    def far_first(n, carry):
        send([(z + 6 - n) % NZ, (z + NZ - 5 + n) % NZ])
        return carry

    lax.fori_loop(0, 6, far_first, 0)
    rc_s[b] = s_s[b]

    for slot in (1, 3, 5, 6, 7):
        halo_wait(slot)
    add = edge_lanes(True)
    for ix in range(ROWS):
        nt_s[pl.ds(ix, C, stride=ROWS), :] = finish_row(ix, add)
    for n in range(8):
        halo_copy(n).wait_send()

    others = pl.ds(0, NB - 1)
    pltpu.make_async_remote_copy(
        s_s.at[others], rc_s.at[others], ssem.at[0], rsem.at[0], device_id=(f, bn), device_id_type=MESH
    ).wait()


def write_kernel(nt_s, rc_s, nt_hbm, ph_hbm, ph_s, sem):
    out_nt = pltpu.make_async_copy(nt_s, nt_hbm, sem.at[0])
    out_nt.start()
    row8 = lax.broadcasted_iota(jnp.int32, (1, 8, LANES), 1)
    lane8 = lax.broadcasted_iota(jnp.int32, (1, 8, LANES), 2)
    outs = []
    for g in range(3):
        grp = pl.ds(16 * g, 16)
        v0, v1 = rc_s[grp, 0:8, :], rc_s[grp, 8:16, :]
        v2 = jnp.concatenate([rc_s[grp, 16:18, :], jnp.zeros((16, 6, LANES), F32)], axis=1)
        a2 = jnp.where(
            row8 < 4, pltpu.roll(v0, 2, 1), jnp.where(row8 < 6, pltpu.roll(v1, 4, 1), pltpu.roll(v2, 6, 1))
        )
        tail = jnp.where(
            lane8 < 32, pltpu.roll(v0, 32, 2), jnp.where(lane8 < 64, pltpu.roll(v1, 64, 2), pltpu.roll(a2, 96, 2))
        )
        v2 = jnp.where(row8 >= 2, tail, v2)
        cols = jnp.concatenate([v0, v1, v2], axis=1).reshape(16 * PEER, LANES)
        part = pl.ds(384 * g, 384)
        ph_s[:, part] = cols.T[:C]
        outs.append(pltpu.make_async_copy(ph_s.at[:, part], ph_hbm.at[:, part], sem.at[1 + g]))
        outs[-1].start()
    for cp in [out_nt] + outs:
        cp.wait()


def on_device(isotope_ratios, advecting_velocity, metric_scaling, thermal_state, outgoing_site_order, daytime_indicator):
    hbm = pl.BlockSpec(memory_space=pltpu.HBM)
    vm = lambda *shape, dtype=F32: pltpu.VMEM(shape, dtype)
    moved = (vm(C * ROWS, LANES), vm(NB, MSG, LANES))
    new_tracers, arrived = pl.pallas_call(
        step_kernel,
        out_shape=moved,
        in_specs=[hbm] * 8,
        out_specs=(pl.BlockSpec(memory_space=pltpu.VMEM),) * 2,
        scratch_shapes=[
            vm(C * ROWS, LANES), vm(2 * LEV * ROWS, LANES), vm(ROWS, LANES), vm(LEV, SITES),
            vm(1, SITES, dtype=jnp.int32), vm(1, SITES, dtype=jnp.int32),
            vm(2 * LANES, 2 * LANES, dtype=BF16), vm(384, 512, dtype=BF16),
            vm(ROWS, CM, LANES), vm(LEV, LANES), vm(2, CM, LANES), vm(6, LEV, LANES),
            vm(12, LEV, LANES), vm(12, 8, LANES),
            vm(SITES, 12 * LANES, dtype=BF16), vm(12 * LANES, 2 * LANES, dtype=BF16),
            vm(NB, MSG, LANES),
            vm(12, 16, LANES), vm(C + LEV + 8, LANES), vm(LANES, LANES),
            pltpu.SemaphoreType.DMA((8,)),
            pltpu.SemaphoreType.DMA((8,)), pltpu.SemaphoreType.DMA((8,)),
            pltpu.SemaphoreType.DMA((1,)), pltpu.SemaphoreType.DMA((1,)),
            pltpu.SemaphoreType.REGULAR((2,)),
        ],
        compiler_params=pltpu.CompilerParams(
            collective_id=0, has_side_effects=True, vmem_limit_bytes=GRANT - 1536 * 1024
        ),
        name="transport_condense",
    )(
        isotope_ratios.reshape(C * ROWS, LANES),
        advecting_velocity.reshape(2 * LEV * ROWS, LANES),
        metric_scaling,
        thermal_state[0],
        outgoing_site_order,
        daytime_indicator,
        jnp.asarray(lane_matrix()),
        jnp.asarray(expand_matrix()),
    )
    new_tracers, physics = pl.pallas_call(
        write_kernel,
        out_shape=(
            jax.ShapeDtypeStruct((C * ROWS, LANES), F32),
            jax.ShapeDtypeStruct((C, SITES), F32),
        ),
        in_specs=(pl.BlockSpec(memory_space=pltpu.VMEM),) * 2,
        out_specs=(hbm, hbm),
        scratch_shapes=[vm(C, SITES), pltpu.SemaphoreType.DMA((4,))],
        compiler_params=pltpu.CompilerParams(vmem_limit_bytes=8 * 1024 * 1024),
        name="write_results",
    )(new_tracers, arrived)
    return (new_tracers.reshape(3, LEV, ROWS, LANES), physics.reshape(1, 3, LEV, SITES))


def solution(mesh):
    placed = (
        P(None, None, "face", "blk"),
        P(None, None, "face", "blk"),
        P("face", "blk"),
        P("face", None, "blk"),
        P("face", "blk"),
        P("face", "blk"),
    )
    return jax.shard_map(
        on_device,
        mesh=mesh,
        in_specs=placed,
        out_specs=(P(None, None, "face", "blk"), P("face", None, None, "blk")),
        check_vma=False,
    )
```
